128 devices in a mesh: section: 4 (over y_lo, core), dp: 32 (over z, x, y_hi).
Axes of the slice: x: 4, y: 4 (y_hi: 2, y_lo: 2; y = y_hi * 2 + y_lo), z: 4, core: 2. Of those that a mesh axis runs over, the one named last changes fastest.
Arguments:
- inputs: bfloat16 [4, 4096, 2048], P(None, 'dp'), may hold values from -6 to 6
- cotangent: bfloat16 [4, 4096, 2048], P(None, 'dp'), may hold values from -0.046875 to 0.046875
- weights: bfloat16 [4, 2048, 2048], P('section'), may hold values from -0.125 to 0.125
- preconds: float32 [4, 32, 64, 64], P('section', 'dp'), may hold values from -0.75 to 0.75
- order: int32 [32, 4], P('dp'), may hold values from 0 to 3, each once within a row
- owner: int32 [32], replicated, may hold values from 0 to 31, each once
Outputs:
- precond: bfloat16 [4, 2048, 2048], P('section')
- gram: float32 [4, 32, 64, 64], P('section', 'dp')
The draws below stay inside these ranges and needn't reach their ends.
Inputs may be any that keep to these rules, and one draw needn't show every extreme that they name: `order`: for each index of dp, each plan slot runs a different micro-batch. `owner`: each device of dp owns exactly one block.
All inputs are finite; a program needn't handle non-finite values.
Results may differ from the reference program's by a relative error of at most 0.013.
Values may be sent and summed in bfloat16 or wider, within the bound.
A program may use at most 128 MiB of HBM per device.

```python
import jax
import jax.numpy as jnp
from jax import lax

D = 2048
MB = 4
TOK = 128
TOKENS = 4096
ROWS = 16384
KB = 64
N_SECTION = 4
N_DP = 32


def levels(stream_key, shape, shards, least, largest):
    gain, own = 1.0, jax.random.fold_in(stream_key, 6)
    for position, parts in shards:
        heights = jnp.exp(jax.random.uniform(jax.random.fold_in(own, position), (parts,), jnp.float32, least / len(shards), largest / len(shards)))
        gain = gain * jnp.repeat(heights, shape[position] // parts).reshape([-1 if axis == position else 1 for axis in range(len(shape))])
    return gain


def gaussian(rng, dims, spread, most, shards=(), kind=jnp.bfloat16):
    values = jax.random.normal(rng, dims, jnp.float32) * spread
    if len(shards) > 0:
        values = levels(rng, dims, shards, -0.22, 0.18) * values
    return jnp.clip(values, min=-most, max=most).astype(kind)


def setup_inputs(seed: int = 0) -> dict:
    streams_of = jax.random.split(jax.random.key(seed), 7)
    return {
        "inputs": gaussian(streams_of[0], (MB, TOKENS, D), 1.0, 6.0, ((1, 32),)),
        "cotangent": gaussian(streams_of[1], (MB, TOKENS, D), (ROWS ** -0.5), 0.046875, ((1, 32),)),
        "weights": gaussian(streams_of[2], (N_SECTION, D, D), D ** -0.5, 0.125, ((0, 4),)),
        "preconds": gaussian(streams_of[3], (N_SECTION, N_DP, KB, KB), KB ** -0.5, 0.75, ((0, 4), (1, 32)), jnp.float32),
        "order": jax.vmap(lambda own: jax.random.permutation(own, MB))(jax.random.split(streams_of[4], N_DP)).reshape((N_DP, MB)).astype(jnp.int32),
        "owner": jax.random.permutation(streams_of[5], N_DP).astype(jnp.int32),
    }


coef = 0.7978845608028654
cubic = 0.044715


def gelu_value(z):
    tanh_part = jnp.tanh(coef * (z + cubic * z * z * z))
    return 0.5 * z * (1.0 + tanh_part)


def gelu_slope(z):
    tanh_part = jnp.tanh(coef * (z + cubic * z * z * z))
    return 0.5 * (1.0 + tanh_part) + 0.5 * z * (1.0 - tanh_part * tanh_part) * coef * (1.0 + 3.0 * cubic * z * z)


def by_device(array):
    width = array.shape[-1]
    return array.reshape(MB, N_DP, TOK, width).transpose(1, 0, 2, 3).reshape(N_DP, MB * TOK, width)


def device_sum(acts, slopes):
    width = acts.shape[-1]
    left = by_device(acts)
    right = by_device(slopes)

    def add_one(total, pair):
        partial_value = lax.dot_general(pair[0], pair[1], (((0,), (0,)), ((), ())), preferred_element_type=jnp.float32)
        rounded = lax.optimization_barrier(partial_value.astype(jnp.bfloat16))
        return total + rounded.astype(jnp.float32), None

    total, _ = lax.scan(add_one, jnp.zeros((width, width), jnp.float32), (left, right))
    return total


def reference(inputs, cotangent, weights, preconds, order, owner):
    width = inputs.shape[-1]
    rows = MB * TOK * N_DP
    split = inputs.reshape(MB, N_DP, TOK, width)
    groups = jnp.arange(N_DP, dtype=jnp.int32)[None, :]
    hidden = split[order.T.astype(jnp.int32), groups].reshape(MB, N_DP * TOK, width)
    saved_in = []
    saved_pre = []
    for section in range(N_SECTION):
        pre = jnp.dot(hidden.reshape(-1, width), weights[section], preferred_element_type=jnp.float32).reshape(hidden.shape)
        saved_in.append(hidden)
        saved_pre.append(pre)
        hidden = (hidden.astype(jnp.float32) + gelu_value(pre)).astype(jnp.bfloat16)
    blocks_of = jnp.zeros((N_DP,), jnp.int32).at[owner].set(jnp.arange(N_DP, dtype=jnp.int32))
    grad_rows = cotangent
    precond_out = [None] * N_SECTION
    gram_out = [None] * N_SECTION
    for section in reversed(range(N_SECTION)):
        acts = saved_in[section]
        slopes = (grad_rows.astype(jnp.float32) * gelu_slope(saved_pre[section])).astype(jnp.bfloat16)
        total = device_sum(acts, slopes)
        mats = preconds[section][owner]
        blocks = total.reshape(N_DP, KB, width)
        result = jnp.einsum("bij,bjn->bin", mats, blocks, precision=lax.Precision.HIGHEST)
        precond_out[section] = result.astype(jnp.bfloat16).reshape(width, width)
        flat = acts.reshape(rows, N_DP, KB).astype(jnp.float32)
        gram_all = jnp.einsum("rbi,rbj->bij", flat, flat, precision=lax.Precision.HIGHEST) / rows
        gram_out[section] = gram_all[blocks_of]
        back = jnp.dot(slopes.reshape(-1, width), weights[section].T, preferred_element_type=jnp.float32).reshape(slopes.shape)
        grad_rows = (grad_rows.astype(jnp.float32) + back).astype(jnp.bfloat16)
    return jnp.stack(precond_out), jnp.stack(gram_out)
```

```python
import functools

import jax
import jax.numpy as jnp
from jax import lax
from jax.experimental import pallas as pl
from jax.experimental.pallas import tpu as pltpu
from jax.sharding import PartitionSpec as P

MESH = pl.DeviceIdType.MESH

coef = 0.7978845608028654
cubic = 0.044715


def passed_along(block, axis, distance):
    devices = range(lax.axis_size(axis))
    route = [(i - distance, i) for i in devices if i - distance in devices]
    return lax.ppermute(block, axis, route)


def gelu_value(z):
    tanh_part = jnp.tanh(coef * (z + cubic * z * z * z))
    return 0.5 * z * (1.0 + tanh_part)


def gelu_slope(z):
    tanh_part = jnp.tanh(coef * (z + cubic * z * z * z))
    return 0.5 * (1.0 + tanh_part) + 0.5 * z * (1.0 - tanh_part * tanh_part) * coef * (
        1.0 + 3.0 * cubic * z * z
    )


WIDE = 512
STAGES = 11


def dp_kernel(
    kinds,
    order,
    blocks_ref,
    h_ref,
    dz_ref,
    pc_ref,
    out_ref,
    gram_ref,
    h_t,
    h_p,
    part,
    from1,
    part2,
    from2,
    last,
    from3,
    full,
    g_part,
    g_from1,
    g_part2,
    g_from2,
    g_last,
    g_from3,
    send1,
    recv1,
    send2,
    recv2,
    send3,
    recv3,
    send4,
    recv4,
    out_sem,
):
    n_chunks = len(kinds)
    me = lax.axis_index("dp")
    my_z, my_x, my_y = me // 8, (me // 2) % 4, me % 2

    def place(z, x, y):
        return z * 8 + x * 2 + y

    rings = {}
    for name, mine in (("x", my_x), ("z", my_z)):
        up, down, far = (mine + 1) % 4, (mine + 3) % 4, (mine + 2) % 4
        if name == "x":
            dev_up, dev_down = place(my_z, up, my_y), place(my_z, down, my_y)
        else:
            dev_up, dev_down = place(up, my_x, my_y), place(down, my_x, my_y)
        rings[name] = (mine, up, down, far, dev_up, dev_down)
    mate = place(my_z, my_x, 1 - my_y)

    barrier = pltpu.get_barrier_semaphore()
    for dev in (rings["x"][4], rings["x"][5], rings["z"][4], rings["z"][5], mate):
        pl.semaphore_signal(barrier, inc=1, device_id={"dp": dev}, device_id_type=MESH)

    def remote(src, dst, send, recv, dev):
        return pltpu.make_async_remote_copy(
            src_ref=src, dst_ref=dst, send_sem=send, recv_sem=recv, device_id={"dp": dev}, device_id_type=MESH
        )

    rows = h_ref.shape[0]
    for tile in range(8):
        block = h_ref[:, tile * 256 : (tile + 1) * 256].T
        h_t[tile * 4 : (tile + 1) * 4] = block.reshape(4, 64, rows)

    def move(p, carry):
        h_p[p // 8, (p // 2) % 4, p % 2] = h_t[blocks_ref[p]]
        return carry

    lax.fori_loop(0, 32, move, 0)

    sent = []

    def start(copy):
        copy.start()
        sent.append(copy)
        return copy

    class Chunk:
        def __init__(self, slot, kind, bufs):
            first, second = ("x", "z") if kind == 0 else ("z", "x")
            self.slot, self.kind = slot, kind
            self.r1, self.r2 = rings[first], rings[second]
            self.part, self.from1, self.part2, self.from2, self.last, self.from3 = bufs
            self.c = {}

        def ring_sends(self, stage, part, landed, send, recv, ring, names):
            mine, up, down, far, dev_up, dev_down = ring
            table = {
                "mp": (far, 0, 0, dev_up),
                "mm": (far, 1, 1, dev_down),
                "dp": (up, 1, 2, dev_up),
                "dm": (down, 0, 3, dev_down),
                "tp": (up, 0, 4, dev_up),
                "tm": (down, 1, 5, dev_down),
            }
            for name in names:
                r, y, k, dev = table[name]
                self.c[stage, name] = start(
                    remote(part.at[r, y], landed.at[k], send.at[self.slot, k], recv.at[self.slot, k], dev)
                )

        def add_far(self, stage, part, landed, ring):
            mine, up, down, far, dev_up, dev_down = ring
            for name, r, y, k in (("mp", up, 0, 0), ("mm", down, 1, 1)):
                self.c[stage, name].wait_recv()
                total = part[r, y].astype(jnp.float32) + landed[k].astype(jnp.float32)
                part[r, y] = total.astype(jnp.bfloat16)

        def sums(self, stage, part, landed, ring):
            for name in ("dp", "dm", "tp", "tm"):
                self.c[stage, name].wait_recv()
            mine = ring[0]
            for y, a, b in ((0, 3, 4), (1, 2, 5)):
                yield y, (
                    part[mine, y].astype(jnp.float32)
                    + landed[a].astype(jnp.float32)
                    + landed[b].astype(jnp.float32)
                )

        def run(self, stage):
            return getattr(self, f"stage{stage}")()

        def product(self, r, y):
            cols = slice(self.slot * WIDE, (self.slot + 1) * WIDE)
            left = h_p[:, r, y] if self.kind == 0 else h_p[r, :, y]
            value = jnp.dot(left.reshape(256, rows), dz_ref[:, cols], preferred_element_type=jnp.float32)
            self.part[r, y] = value.astype(jnp.bfloat16).reshape(4, 64, WIDE)

        def stage0(self):
            mine, up, down, far = self.r1[:4]
            args = (1, self.part, self.from1, send1, recv1, self.r1)
            self.product(far, 0)
            self.ring_sends(*args, ("mp",))
            self.product(far, 1)
            self.ring_sends(*args, ("mm",))
            self.product(up, 1)
            self.ring_sends(*args, ("dp",))
            self.product(down, 0)
            self.ring_sends(*args, ("dm",))
            self.product(up, 0)
            self.product(down, 1)

        def stage1(self):
            self.add_far(1, self.part, self.from1, self.r1)
            self.ring_sends(1, self.part, self.from1, send1, recv1, self.r1, ("tp", "tm"))
            self.product(self.r1[0], 0)
            self.product(self.r1[0], 1)

        def stage2(self):
            for y, total in self.sums(1, self.part, self.from1, self.r1):
                for r in range(4):
                    self.part2[r, y] = total[r].astype(jnp.bfloat16)
            self.ring_sends(2, self.part2, self.from2, send2, recv2, self.r2, ("mp", "mm", "dp", "dm"))

        def stage3(self):
            self.add_far(2, self.part2, self.from2, self.r2)
            self.ring_sends(2, self.part2, self.from2, send2, recv2, self.r2, ("tp", "tm"))

        def stage4(self):
            for y, total in self.sums(2, self.part2, self.from2, self.r2):
                self.last[y] = total.astype(jnp.bfloat16)
            self.c["y"] = start(
                remote(self.last.at[1 - my_y], self.from3, send3.at[self.slot], recv3.at[self.slot], mate)
            )

        def total(self):
            self.c["y"].wait_recv()
            return self.last[my_y].astype(jnp.float32) + self.from3[...].astype(jnp.float32)

        def gather(self, name, k, where, dev):
            ref = full.at[self.slot].at[where]
            self.c["g", name] = start(
                remote(ref, ref, send4.at[self.slot, k], recv4.at[self.slot, k], dev)
            )

        def stage5(self):
            done = jnp.dot(
                pc_ref[...], self.total(), precision=lax.Precision.HIGHEST, preferred_element_type=jnp.float32
            )
            m1, m2 = self.r1[0], self.r2[0]
            full[self.slot, m1, m2, my_y] = done.astype(jnp.bfloat16)
            self.gather("y", 0, (m1, m2, my_y), mate)

        def stage6(self):
            self.c["g", "y"].wait_recv()
            m1, m2 = self.r1[0], self.r2[0]
            self.gather("2p", 1, (m1, m2), self.r2[4])
            self.gather("2m", 2, (m1, m2), self.r2[5])

        def stage7(self):
            m1 = self.r1[0]
            self.c["g", "2p"].wait_recv()
            self.gather("f2p", 3, (m1, self.r2[2], 0), self.r2[4])
            self.c["g", "2m"].wait_recv()
            self.gather("f2m", 4, (m1, self.r2[1], 1), self.r2[5])

        def stage8(self):
            self.c["g", "f2p"].wait_recv()
            self.c["g", "f2m"].wait_recv()
            self.gather("1p", 5, (self.r1[0],), self.r1[4])
            self.gather("1m", 6, (self.r1[0],), self.r1[5])

        def stage9(self):
            self.c["g", "1p"].wait_recv()
            self.gather("f1p", 7, (self.r1[2], slice(None), 0), self.r1[4])
            self.c["g", "1m"].wait_recv()
            self.gather("f1m", 8, (self.r1[1], slice(None), 1), self.r1[5])

        def stage10(self):
            self.c["g", "f1p"].wait_recv()
            self.c["g", "f1m"].wait_recv()
            copy = pltpu.make_async_copy(full.at[self.slot], out_ref.at[self.slot], out_sem.at[self.slot])
            copy.start()
            self.out = copy

    g_part[...] = jnp.zeros(g_part.shape, g_part.dtype)
    for z in range(4):
        for half in range(2):
            left = h_p[z, half * 2 : half * 2 + 2].reshape(256, rows)
            square = lax.dot_general(left, left, (((1,), (1,)), ((), ())), preferred_element_type=jnp.float32)
            for k in range(4):
                lanes = slice(k * 64, (k + 1) * 64)
                g_part[half * 2 + k // 2, k % 2, z, :, 0:64] = square[lanes, lanes].astype(jnp.bfloat16)
    pl.semaphore_wait(barrier, 5)

    g_bufs = (g_part, g_from1, g_part2, g_from2, g_last, g_from3)
    gram = Chunk(n_chunks, 0, g_bufs)
    gram.ring_sends(1, g_part, g_from1, send1, recv1, gram.r1, ("mp", "mm", "dp", "dm"))

    def gram_stage1():
        gram.add_far(1, g_part, g_from1, gram.r1)
        gram.ring_sends(1, g_part, g_from1, send1, recv1, gram.r1, ("tp", "tm"))

    def gram_stage5():
        gram_ref[...] = gram.total()[:, 0:64] * (1.0 / 16384.0)

    gram_stages = {1: gram_stage1, 2: gram.stage2, 3: gram.stage3, 4: gram.stage4, 5: gram_stage5}
    chunks = []
    for slot, kind in enumerate(kinds):
        bufs = tuple(ref.at[slot] for ref in (part, from1, part2, from2, last, from3))
        chunks.append(Chunk(slot, kind, bufs))
    for slot, stage in order:
        if slot == n_chunks:
            gram_stages[stage]()
        else:
            chunks[slot].run(stage)
    for copy in sent:
        copy.wait_send()
    for chunk in chunks:
        chunk.out.wait()


def dp_order(n_chunks, lag):
    order = []
    for step in range(STAGES + lag * (n_chunks // 2 - 1)):
        for slot in range(n_chunks):
            stage = step - lag * (slot // 2)
            if 0 <= stage < STAGES:
                order.append((slot, stage))
        if 0 <= step < 5:
            order.append((n_chunks, step + 1))
    return tuple(order)


KINDS = (0, 1, 0, 1)
LAG = 2


def dp_part(acts, slopes, precond, blocks_of):
    n = len(KINDS)
    rows, width = acts.shape
    bf = jnp.bfloat16
    vmem = pl.BlockSpec(memory_space=pltpu.VMEM)

    def ring_scratch(lead, wide):
        return [
            pltpu.VMEM((*lead, 4, 2, 4, 64, wide), bf),
            pltpu.VMEM((*lead, 6, 4, 64, wide), bf),
            pltpu.VMEM((*lead, 4, 2, 64, wide), bf),
            pltpu.VMEM((*lead, 6, 64, wide), bf),
            pltpu.VMEM((*lead, 2, 64, wide), bf),
            pltpu.VMEM((*lead, 64, wide), bf),
        ]

    dma = pltpu.SemaphoreType.DMA
    return pl.pallas_call(
        functools.partial(dp_kernel, KINDS, dp_order(n, LAG)),
        out_shape=(
            jax.ShapeDtypeStruct((n, 4, 4, 2, 64, WIDE), bf),
            jax.ShapeDtypeStruct((64, 64), jnp.float32),
        ),
        in_specs=[pl.BlockSpec(memory_space=pltpu.SMEM), vmem, vmem, vmem],
        out_specs=(pl.BlockSpec(memory_space=pl.ANY), vmem),
        scratch_shapes=[
            pltpu.VMEM((32, 64, rows), bf),
            pltpu.VMEM((4, 4, 2, 64, rows), bf),
            *ring_scratch((n,), WIDE),
            pltpu.VMEM((n, 4, 4, 2, 64, WIDE), bf),
            *ring_scratch((), 128),
            dma((n + 1, 6)),
            dma((n + 1, 6)),
            dma((n + 1, 6)),
            dma((n + 1, 6)),
            dma((n + 1,)),
            dma((n + 1,)),
            dma((n, 9)),
            dma((n, 9)),
            dma((n,)),
        ],
        compiler_params=pltpu.CompilerParams(
            collective_id=1, has_side_effects=True, vmem_limit_bytes=60 * 1024 * 1024
        ),
        name="dp_part",
    )(blocks_of, acts, slopes, precond)


def restore_kernel(owner_ref, src_ref, dst_ref, held, in_sem, out_sem):
    n = len(KINDS)

    def fetch(b, c):
        o = owner_ref[b]
        z, x, y = o // 8, (o // 2) % 4, o % 2
        where = (x, z, y) if KINDS[c] == 0 else (z, x, y)
        return pltpu.make_async_copy(
            src_ref.at[(c, *where)], held.at[b, :, pl.ds(c * WIDE, WIDE)], in_sem.at[b, c]
        )

    def first(b, carry):
        for c in range(n):
            fetch(b, c).start()
        return carry

    def put(b):
        return pltpu.make_async_copy(held.at[b], dst_ref.at[b], out_sem.at[b])

    def second(b, carry):
        for c in range(n):
            fetch(b, c).wait()
        put(b).start()
        return carry

    def third(b, carry):
        put(b).wait()
        return carry

    lax.fori_loop(0, 32, first, 0)
    lax.fori_loop(0, 32, second, 0)
    lax.fori_loop(0, 32, third, 0)


def restore(gathered, owner):
    n = len(KINDS)
    return pl.pallas_call(
        restore_kernel,
        out_shape=jax.ShapeDtypeStruct((32, 64, n * WIDE), jnp.bfloat16),
        in_specs=[pl.BlockSpec(memory_space=pltpu.SMEM), pl.BlockSpec(memory_space=pl.ANY)],
        out_specs=pl.BlockSpec(memory_space=pl.ANY),
        scratch_shapes=[
            pltpu.VMEM((32, 64, n * WIDE), jnp.bfloat16),
            pltpu.SemaphoreType.DMA((32, n)),
            pltpu.SemaphoreType.DMA((32,)),
        ],
        compiler_params=pltpu.CompilerParams(vmem_limit_bytes=40 * 1024 * 1024),
        name="restore",
    )(owner, gathered)


def body(inputs, cotangent, weights, preconds, order, owner):
    weight = weights[0]
    sections = lax.axis_size("section")
    place = lax.axis_index("section")
    n_micro = inputs.shape[0]
    tok_rows = inputs.shape[1]
    width = inputs.shape[2]
    n_group = owner.shape[0]
    block = width // n_group
    total_rows = n_micro * tok_rows * n_group
    n_steps = n_micro + sections - 1
    feed = jnp.take(inputs, order[0], axis=0)
    saved_in = jnp.zeros((n_micro, tok_rows, width), jnp.bfloat16)
    saved_pre = jnp.zeros((n_micro, tok_rows, width), jnp.float32)

    def forward_step(carry, step):
        incoming, kept_in, kept_pre = carry
        slot = step - place
        valid = (slot >= 0) & (slot < n_micro)
        slot_c = jnp.clip(slot, 0, n_micro - 1)
        first = lax.dynamic_index_in_dim(feed, slot_c, 0, keepdims=False)
        current = jnp.where(place == 0, first, incoming)
        pre = jnp.dot(current, weight, preferred_element_type=jnp.float32)
        output = (current.astype(jnp.float32) + gelu_value(pre)).astype(jnp.bfloat16)
        old_in = lax.dynamic_index_in_dim(kept_in, slot_c, 0, keepdims=False)
        kept_in = lax.dynamic_update_index_in_dim(
            kept_in, jnp.where(valid, current, old_in), slot_c, 0
        )
        old_pre = lax.dynamic_index_in_dim(kept_pre, slot_c, 0, keepdims=False)
        kept_pre = lax.dynamic_update_index_in_dim(
            kept_pre, jnp.where(valid, pre, old_pre), slot_c, 0
        )
        incoming = passed_along(output, "section", 1)
        return ((incoming, kept_in, kept_pre), None)

    start_rows = jnp.zeros((tok_rows, width), jnp.bfloat16)
    (unused_rows, saved_in, saved_pre), _ = lax.scan(
        forward_step, (start_rows, saved_in, saved_pre), jnp.arange(n_steps, dtype=jnp.int32)
    )

    def backward_step(carry, step):
        incoming, kept = carry
        slot = step - (sections - 1 - place)
        valid = (slot >= 0) & (slot < n_micro)
        slot_c = jnp.clip(slot, 0, n_micro - 1)
        last = lax.dynamic_index_in_dim(cotangent, slot_c, 0, keepdims=False)
        current = jnp.where(place == sections - 1, last, incoming)
        current = jnp.where(valid, current, jnp.zeros_like(current))
        acts = lax.dynamic_index_in_dim(saved_in, slot_c, 0, keepdims=False)
        pre = lax.dynamic_index_in_dim(saved_pre, slot_c, 0, keepdims=False)
        slopes = (current.astype(jnp.float32) * gelu_slope(pre)).astype(jnp.bfloat16)
        old = lax.dynamic_index_in_dim(kept, slot_c, 0, keepdims=False)
        kept = lax.dynamic_update_index_in_dim(kept, jnp.where(valid, slopes, old), slot_c, 0)
        back = lax.dot_general(
            slopes, weight, (((1,), (1,)), ((), ())), preferred_element_type=jnp.float32
        )
        sent = (current.astype(jnp.float32) + back).astype(jnp.bfloat16)
        incoming = passed_along(sent, "section", -1)
        return ((incoming, kept), None)

    kept = jnp.zeros_like(saved_in)
    (unused_back, kept), _ = lax.scan(
        backward_step, (start_rows, kept), jnp.arange(n_steps, dtype=jnp.int32)
    )
    positions = jnp.arange(n_group, dtype=jnp.int32)
    matches = (owner[None, :] == positions[:, None]).astype(jnp.int32)
    blocks_of = jnp.sum(matches * positions[None, :], axis=1)
    gathered, gram = dp_part(
        saved_in.reshape(-1, width), kept.reshape(-1, width), preconds[0, 0], blocks_of
    )
    result = restore(gathered, owner).reshape(1, width, width)
    return (result, gram.reshape(1, 1, block, block))


def solution(mesh):
    placed = (
        P(None, "dp", None),
        P(None, "dp", None),
        P("section", None, None),
        P("section", "dp", None, None),
        P("dp", None),
        P(),
    )
    return jax.shard_map(
        body,
        mesh=mesh,
        in_specs=placed,
        out_specs=(P("section", None, None), P("section", "dp", None, None)),
        check_vma=False,
    )
```

```python
import functools

import jax
import jax.numpy as jnp
from jax import lax
from jax.experimental import pallas as pl
from jax.experimental.pallas import tpu as pltpu
from jax.sharding import PartitionSpec as P

MESH = pl.DeviceIdType.MESH
coef = 0.7978845608028654
cubic = 0.044715


TILE = 512


def relay_kernel(
    order_ref,
    inputs_ref,
    cot_ref,
    weight_ref,
    acts_ref,
    slopes_ref,
    w,
    feed,
    held,
    slope,
    onward,
    grads,
    dz,
    back,
    w_sem,
    in_sem,
    out_sem,
    f_send,
    f_recv,
    b_send,
    b_recv,
):
    s = lax.axis_index("section")
    n_micro, rows, width = held.shape
    n_tiles = width // TILE
    last = 3

    barrier = pltpu.get_barrier_semaphore()
    for dev in ((s + 1) % 4, (s + 3) % 4):
        pl.semaphore_signal(barrier, inc=1, device_id={"section": dev}, device_id_type=MESH)

    def columns(t):
        return slice(t * TILE, (t + 1) * TILE)

    def w_copy(t):
        return pltpu.make_async_copy(weight_ref.at[0, :, columns(t)], w.at[:, columns(t)], w_sem.at[t])

    feed_copy = pltpu.make_async_copy(inputs_ref, feed, in_sem)
    cot_copy = pltpu.make_async_copy(cot_ref, grads, in_sem)

    @pl.when(s == 0)
    def _():
        feed_copy.start()

    for t in range(n_tiles):
        w_copy(t).start()

    @pl.when(s == last)
    def _():
        cot_copy.start()

    pl.semaphore_wait(barrier, 2)

    @pl.when(s == 0)
    def _():
        feed_copy.wait()

    @pl.when(s == last)
    def _():
        cot_copy.wait()

    def forward_copy(k, t):
        return pltpu.make_async_remote_copy(
            src_ref=onward.at[k, :, columns(t)],
            dst_ref=held.at[k, :, columns(t)],
            send_sem=f_send.at[k, t],
            recv_sem=f_recv.at[k, t],
            device_id={"section": (s + 1) % 4},
            device_id_type=MESH,
        )

    def backward_copy(k, t):
        return pltpu.make_async_remote_copy(
            src_ref=back.at[k, :, columns(t)],
            dst_ref=grads.at[k, :, columns(t)],
            send_sem=b_send.at[k, t],
            recv_sem=b_recv.at[k, t],
            device_id={"section": (s + 3) % 4},
            device_id_type=MESH,
        )

    def acts_copy(k):
        return pltpu.make_async_copy(held.at[k], acts_ref.at[k], out_sem.at[0, k])

    def slopes_copy(k):
        return pltpu.make_async_copy(dz.at[k], slopes_ref.at[k], out_sem.at[1, k])

    def forward(k):
        @pl.when(s == 0)
        def _():
            held[k] = feed[order_ref[k]]

        @pl.when(s > 0)
        def _():
            for t in range(n_tiles):
                forward_copy(k, t).wait_recv()

        acts_copy(k).start()
        for t in range(n_tiles):

            @pl.when(k == 0)
            def _():
                w_copy(t).wait()

            z = jnp.dot(held[k], w[:, columns(t)], preferred_element_type=jnp.float32)
            square = z * z
            tanh_part = jnp.tanh(coef * (z + cubic * square * z))
            half = 0.5 * (1.0 + tanh_part)
            slope[k, :, columns(t)] = half + 0.5 * z * (1.0 - tanh_part * tanh_part) * coef * (
                1.0 + 3.0 * cubic * square
            )

            @pl.when(s < last)
            def _():
                before = held[k, :, columns(t)].astype(jnp.float32)
                onward[k, :, columns(t)] = (before + z * half).astype(jnp.bfloat16)
                forward_copy(k, t).start()

    def backward(k):
        @pl.when(s < last)
        def _():
            for t in range(n_tiles):
                backward_copy(k, t).wait_recv()

        for t in range(n_tiles):
            g = grads[k, :, columns(t)].astype(jnp.float32)
            dz[k, :, columns(t)] = (g * slope[k, :, columns(t)]).astype(jnp.bfloat16)
        slopes_copy(k).start()

        @pl.when(s > 0)
        def _():
            for t in range(n_tiles):
                value = lax.dot_general(
                    dz[k],
                    w[columns(t), :],
                    (((1,), (1,)), ((), ())),
                    preferred_element_type=jnp.float32,
                )
                g = grads[k, :, columns(t)].astype(jnp.float32)
                back[k, :, columns(t)] = (g + value).astype(jnp.bfloat16)
                backward_copy(k, t).start()

    def step(k, carry):
        @pl.when(k < n_micro)
        def _():
            forward(k)

        b = k - (last - s)

        @pl.when((b >= 0) & (b < n_micro))
        def _():
            backward(b)

        return carry

    lax.fori_loop(0, n_micro + last, step, 0)

    def drain(k, carry):
        acts_copy(k).wait()
        slopes_copy(k).wait()

        @pl.when(s < last)
        def _():
            for t in range(n_tiles):
                forward_copy(k, t).wait_send()

        @pl.when(s > 0)
        def _():
            for t in range(n_tiles):
                backward_copy(k, t).wait_send()

        return carry

    lax.fori_loop(0, n_micro, drain, 0)


def relay(inputs, cotangent, weights, order):
    n_micro, rows, width = inputs.shape
    n_tiles = width // TILE
    bf = jnp.bfloat16
    hbm = pl.BlockSpec(memory_space=pl.ANY)
    block = pltpu.VMEM((n_micro, rows, width), bf)
    dma = pltpu.SemaphoreType.DMA
    out = jax.ShapeDtypeStruct((n_micro, rows, width), bf)
    return pl.pallas_call(
        relay_kernel,
        out_shape=(out, out),
        in_specs=[pl.BlockSpec(memory_space=pltpu.SMEM), hbm, hbm, hbm],
        out_specs=(hbm, hbm),
        scratch_shapes=[
            pltpu.VMEM((width, width), bf),
            block,
            block,
            pltpu.VMEM((n_micro, rows, width), jnp.float32),
            block,
            block,
            block,
            block,
            dma((n_tiles,)),
            dma(()),
            dma((2, n_micro)),
            dma((n_micro, n_tiles)),
            dma((n_micro, n_tiles)),
            dma((n_micro, n_tiles)),
            dma((n_micro, n_tiles)),
        ],
        compiler_params=pltpu.CompilerParams(
            collective_id=0, has_side_effects=True, vmem_limit_bytes=60 * 1024 * 1024
        ),
        name="relay",
    )(order, inputs, cotangent, weights)


WIDE = 512
STAGES = 11


def dp_kernel(
    kinds,
    order,
    blocks_ref,
    h_ref,
    dz_ref,
    pc_ref,
    out_ref,
    gram_ref,
    h_t,
    h_p,
    part,
    from1,
    part2,
    from2,
    last,
    from3,
    full,
    g_part,
    g_from1,
    g_part2,
    g_from2,
    g_last,
    g_from3,
    send1,
    recv1,
    send2,
    recv2,
    send3,
    recv3,
    send4,
    recv4,
    out_sem,
):
    n_chunks = len(kinds)
    me = lax.axis_index("dp")
    my_z, my_x, my_y = me // 8, (me // 2) % 4, me % 2

    def place(z, x, y):
        return z * 8 + x * 2 + y

    rings = {}
    for name, mine in (("x", my_x), ("z", my_z)):
        up, down, far = (mine + 1) % 4, (mine + 3) % 4, (mine + 2) % 4
        if name == "x":
            dev_up, dev_down = place(my_z, up, my_y), place(my_z, down, my_y)
        else:
            dev_up, dev_down = place(up, my_x, my_y), place(down, my_x, my_y)
        rings[name] = (mine, up, down, far, dev_up, dev_down)
    mate = place(my_z, my_x, 1 - my_y)

    barrier = pltpu.get_barrier_semaphore()
    for dev in (rings["x"][4], rings["x"][5], rings["z"][4], rings["z"][5], mate):
        pl.semaphore_signal(barrier, inc=1, device_id={"dp": dev}, device_id_type=MESH)

    def remote(src, dst, send, recv, dev):
        return pltpu.make_async_remote_copy(
            src_ref=src, dst_ref=dst, send_sem=send, recv_sem=recv, device_id={"dp": dev}, device_id_type=MESH
        )

    rows = h_ref.shape[0]
    for tile in range(8):
        block = h_ref[:, tile * 256 : (tile + 1) * 256].T
        h_t[tile * 4 : (tile + 1) * 4] = block.reshape(4, 64, rows)

    def move(p, carry):
        h_p[p // 8, (p // 2) % 4, p % 2] = h_t[blocks_ref[p]]
        return carry

    lax.fori_loop(0, 32, move, 0)

    sent = []

    def start(copy):
        copy.start()
        sent.append(copy)
        return copy

    class Chunk:
        def __init__(self, slot, kind, bufs):
            first, second = ("x", "z") if kind == 0 else ("z", "x")
            self.slot, self.kind = slot, kind
            self.r1, self.r2 = rings[first], rings[second]
            self.part, self.from1, self.part2, self.from2, self.last, self.from3 = bufs
            self.c = {}

        def ring_sends(self, stage, part, landed, send, recv, ring, names):
            mine, up, down, far, dev_up, dev_down = ring
            table = {
                "mp": (far, 0, 0, dev_up),
                "mm": (far, 1, 1, dev_down),
                "dp": (up, 1, 2, dev_up),
                "dm": (down, 0, 3, dev_down),
                "tp": (up, 0, 4, dev_up),
                "tm": (down, 1, 5, dev_down),
            }
            for name in names:
                r, y, k, dev = table[name]
                self.c[stage, name] = start(
                    remote(part.at[r, y], landed.at[k], send.at[self.slot, k], recv.at[self.slot, k], dev)
                )

        def add_far(self, stage, part, landed, ring):
            mine, up, down, far, dev_up, dev_down = ring
            for name, r, y, k in (("mp", up, 0, 0), ("mm", down, 1, 1)):
                self.c[stage, name].wait_recv()
                total = part[r, y].astype(jnp.float32) + landed[k].astype(jnp.float32)
                part[r, y] = total.astype(jnp.bfloat16)

        def sums(self, stage, part, landed, ring):
            for name in ("dp", "dm", "tp", "tm"):
                self.c[stage, name].wait_recv()
            mine = ring[0]
            for y, a, b in ((0, 3, 4), (1, 2, 5)):
                yield y, (
                    part[mine, y].astype(jnp.float32)
                    + landed[a].astype(jnp.float32)
                    + landed[b].astype(jnp.float32)
                )

        def run(self, stage):
            return getattr(self, f"stage{stage}")()

        def product(self, r, y):
            cols = slice(self.slot * WIDE, (self.slot + 1) * WIDE)
            left = h_p[:, r, y] if self.kind == 0 else h_p[r, :, y]
            value = jnp.dot(left.reshape(256, rows), dz_ref[:, cols], preferred_element_type=jnp.float32)
            self.part[r, y] = value.astype(jnp.bfloat16).reshape(4, 64, WIDE)

        def stage0(self):
            mine, up, down, far = self.r1[:4]
            args = (1, self.part, self.from1, send1, recv1, self.r1)
            self.product(far, 0)
            self.ring_sends(*args, ("mp",))
            self.product(far, 1)
            self.ring_sends(*args, ("mm",))
            self.product(up, 1)
            self.ring_sends(*args, ("dp",))
            self.product(down, 0)
            self.ring_sends(*args, ("dm",))
            self.product(up, 0)
            self.product(down, 1)

        def stage1(self):
            self.add_far(1, self.part, self.from1, self.r1)
            self.ring_sends(1, self.part, self.from1, send1, recv1, self.r1, ("tp", "tm"))
            self.product(self.r1[0], 0)
            self.product(self.r1[0], 1)

        def stage2(self):
            for y, total in self.sums(1, self.part, self.from1, self.r1):
                for r in range(4):
                    self.part2[r, y] = total[r].astype(jnp.bfloat16)
            self.ring_sends(2, self.part2, self.from2, send2, recv2, self.r2, ("mp", "mm", "dp", "dm"))

        def stage3(self):
            self.add_far(2, self.part2, self.from2, self.r2)
            self.ring_sends(2, self.part2, self.from2, send2, recv2, self.r2, ("tp", "tm"))

        def stage4(self):
            for y, total in self.sums(2, self.part2, self.from2, self.r2):
                self.last[y] = total.astype(jnp.bfloat16)
            self.c["y"] = start(
                remote(self.last.at[1 - my_y], self.from3, send3.at[self.slot], recv3.at[self.slot], mate)
            )

        def total(self):
            self.c["y"].wait_recv()
            return self.last[my_y].astype(jnp.float32) + self.from3[...].astype(jnp.float32)

        def gather(self, name, k, where, dev):
            ref = full.at[self.slot].at[where]
            self.c["g", name] = start(
                remote(ref, ref, send4.at[self.slot, k], recv4.at[self.slot, k], dev)
            )

        def stage5(self):
            done = jnp.dot(
                pc_ref[...], self.total(), precision=lax.Precision.HIGHEST, preferred_element_type=jnp.float32
            )
            m1, m2 = self.r1[0], self.r2[0]
            full[self.slot, m1, m2, my_y] = done.astype(jnp.bfloat16)
            self.gather("y", 0, (m1, m2, my_y), mate)

        def stage6(self):
            self.c["g", "y"].wait_recv()
            m1, m2 = self.r1[0], self.r2[0]
            self.gather("2p", 1, (m1, m2), self.r2[4])
            self.gather("2m", 2, (m1, m2), self.r2[5])

        def stage7(self):
            m1 = self.r1[0]
            self.c["g", "2p"].wait_recv()
            self.gather("f2p", 3, (m1, self.r2[2], 0), self.r2[4])
            self.c["g", "2m"].wait_recv()
            self.gather("f2m", 4, (m1, self.r2[1], 1), self.r2[5])

        def stage8(self):
            self.c["g", "f2p"].wait_recv()
            self.c["g", "f2m"].wait_recv()
            self.gather("1p", 5, (self.r1[0],), self.r1[4])
            self.gather("1m", 6, (self.r1[0],), self.r1[5])

        def stage9(self):
            self.c["g", "1p"].wait_recv()
            self.gather("f1p", 7, (self.r1[2], slice(None), 0), self.r1[4])
            self.c["g", "1m"].wait_recv()
            self.gather("f1m", 8, (self.r1[1], slice(None), 1), self.r1[5])

        def stage10(self):
            self.c["g", "f1p"].wait_recv()
            self.c["g", "f1m"].wait_recv()
            copy = pltpu.make_async_copy(full.at[self.slot], out_ref.at[self.slot], out_sem.at[self.slot])
            copy.start()
            self.out = copy

    g_part[...] = jnp.zeros(g_part.shape, g_part.dtype)
    for z in range(4):
        for half in range(2):
            left = h_p[z, half * 2 : half * 2 + 2].reshape(256, rows)
            square = lax.dot_general(left, left, (((1,), (1,)), ((), ())), preferred_element_type=jnp.float32)
            for k in range(4):
                lanes = slice(k * 64, (k + 1) * 64)
                g_part[half * 2 + k // 2, k % 2, z, :, 0:64] = square[lanes, lanes].astype(jnp.bfloat16)
    pl.semaphore_wait(barrier, 5)

    g_bufs = (g_part, g_from1, g_part2, g_from2, g_last, g_from3)
    gram = Chunk(n_chunks, 0, g_bufs)
    gram.ring_sends(1, g_part, g_from1, send1, recv1, gram.r1, ("mp", "mm", "dp", "dm"))

    def gram_stage1():
        gram.add_far(1, g_part, g_from1, gram.r1)
        gram.ring_sends(1, g_part, g_from1, send1, recv1, gram.r1, ("tp", "tm"))

    def gram_stage5():
        gram_ref[...] = gram.total()[:, 0:64] * (1.0 / 16384.0)

    gram_stages = {1: gram_stage1, 2: gram.stage2, 3: gram.stage3, 4: gram.stage4, 5: gram_stage5}
    chunks = []
    for slot, kind in enumerate(kinds):
        bufs = tuple(ref.at[slot] for ref in (part, from1, part2, from2, last, from3))
        chunks.append(Chunk(slot, kind, bufs))
    for slot, stage in order:
        if slot == n_chunks:
            gram_stages[stage]()
        else:
            chunks[slot].run(stage)
    for copy in sent:
        copy.wait_send()
    for chunk in chunks:
        chunk.out.wait()


def dp_order(n_chunks, lag):
    order = []
    for step in range(STAGES + lag * (n_chunks // 2 - 1)):
        for slot in range(n_chunks):
            stage = step - lag * (slot // 2)
            if 0 <= stage < STAGES:
                order.append((slot, stage))
        if 0 <= step < 5:
            order.append((n_chunks, step + 1))
    return tuple(order)


KINDS = (0, 1, 0, 1)
LAG = 2


def dp_part(acts, slopes, precond, blocks_of):
    n = len(KINDS)
    rows, width = acts.shape
    bf = jnp.bfloat16
    vmem = pl.BlockSpec(memory_space=pltpu.VMEM)

    def ring_scratch(lead, wide):
        return [
            pltpu.VMEM((*lead, 4, 2, 4, 64, wide), bf),
            pltpu.VMEM((*lead, 6, 4, 64, wide), bf),
            pltpu.VMEM((*lead, 4, 2, 64, wide), bf),
            pltpu.VMEM((*lead, 6, 64, wide), bf),
            pltpu.VMEM((*lead, 2, 64, wide), bf),
            pltpu.VMEM((*lead, 64, wide), bf),
        ]

    dma = pltpu.SemaphoreType.DMA
    return pl.pallas_call(
        functools.partial(dp_kernel, KINDS, dp_order(n, LAG)),
        out_shape=(
            jax.ShapeDtypeStruct((n, 4, 4, 2, 64, WIDE), bf),
            jax.ShapeDtypeStruct((64, 64), jnp.float32),
        ),
        in_specs=[pl.BlockSpec(memory_space=pltpu.SMEM), vmem, vmem, vmem],
        out_specs=(pl.BlockSpec(memory_space=pl.ANY), vmem),
        scratch_shapes=[
            pltpu.VMEM((32, 64, rows), bf),
            pltpu.VMEM((4, 4, 2, 64, rows), bf),
            *ring_scratch((n,), WIDE),
            pltpu.VMEM((n, 4, 4, 2, 64, WIDE), bf),
            *ring_scratch((), 128),
            dma((n + 1, 6)),
            dma((n + 1, 6)),
            dma((n + 1, 6)),
            dma((n + 1, 6)),
            dma((n + 1,)),
            dma((n + 1,)),
            dma((n, 9)),
            dma((n, 9)),
            dma((n,)),
        ],
        compiler_params=pltpu.CompilerParams(
            collective_id=1, has_side_effects=True, vmem_limit_bytes=60 * 1024 * 1024
        ),
        name="dp_part",
    )(blocks_of, acts, slopes, precond)


def restore_kernel(owner_ref, src_ref, dst_ref, held, in_sem, out_sem):
    n = len(KINDS)

    def fetch(b, c):
        o = owner_ref[b]
        z, x, y = o // 8, (o // 2) % 4, o % 2
        where = (x, z, y) if KINDS[c] == 0 else (z, x, y)
        return pltpu.make_async_copy(
            src_ref.at[(c, *where)], held.at[b, :, pl.ds(c * WIDE, WIDE)], in_sem.at[b, c]
        )

    def first(b, carry):
        for c in range(n):
            fetch(b, c).start()
        return carry

    def put(b):
        return pltpu.make_async_copy(held.at[b], dst_ref.at[b], out_sem.at[b])

    def second(b, carry):
        for c in range(n):
            fetch(b, c).wait()
        put(b).start()
        return carry

    def third(b, carry):
        put(b).wait()
        return carry

    lax.fori_loop(0, 32, first, 0)
    lax.fori_loop(0, 32, second, 0)
    lax.fori_loop(0, 32, third, 0)


def restore(gathered, owner):
    n = len(KINDS)
    return pl.pallas_call(
        restore_kernel,
        out_shape=jax.ShapeDtypeStruct((32, 64, n * WIDE), jnp.bfloat16),
        in_specs=[pl.BlockSpec(memory_space=pltpu.SMEM), pl.BlockSpec(memory_space=pl.ANY)],
        out_specs=pl.BlockSpec(memory_space=pl.ANY),
        scratch_shapes=[
            pltpu.VMEM((32, 64, n * WIDE), jnp.bfloat16),
            pltpu.SemaphoreType.DMA((32, n)),
            pltpu.SemaphoreType.DMA((32,)),
        ],
        compiler_params=pltpu.CompilerParams(vmem_limit_bytes=40 * 1024 * 1024),
        name="restore",
    )(owner, gathered)


def body(inputs, cotangent, weights, preconds, order, owner):
    width = inputs.shape[2]
    n_group = owner.shape[0]
    acts, slopes = relay(inputs, cotangent, weights, order[0])
    positions = jnp.arange(n_group, dtype=jnp.int32)
    matches = (owner[None, :] == positions[:, None]).astype(jnp.int32)
    blocks_of = jnp.sum(matches * positions[None, :], axis=1)
    gathered, gram = dp_part(
        acts.reshape(-1, width), slopes.reshape(-1, width), preconds[0, 0], blocks_of
    )
    result = restore(gathered, owner).reshape(1, width, width)
    return (result, gram.reshape(1, 1, *gram.shape))


def solution(mesh):
    placed = (
        P(None, "dp", None),
        P(None, "dp", None),
        P("section", None, None),
        P("section", "dp", None, None),
        P("dp", None),
        P(),
    )
    return jax.shard_map(
        body,
        mesh=mesh,
        in_specs=placed,
        out_specs=(P("section", None, None), P("section", "dp", None, None)),
        check_vma=False,
    )
```

```python
import functools

import jax
import jax.numpy as jnp
from jax import lax
from jax.experimental import pallas as pl
from jax.experimental.pallas import tpu as pltpu
from jax.sharding import PartitionSpec as P

MESH = pl.DeviceIdType.MESH
coef = 0.7978845608028654
cubic = 0.044715


TILE = 512


def relay_kernel(
    order_ref,
    blocks_ref,
    inputs_ref,
    cot_ref,
    weight_ref,
    turned_ref,
    dz,
    g_part,
    w,
    feed,
    held,
    slope,
    onward,
    grads,
    back,
    total,
    flipped,
    w_sem,
    in_sem,
    f_send,
    f_recv,
    b_send,
    b_recv,
):
    s = lax.axis_index("section")
    n_micro, rows, width = held.shape
    n_tiles = width // TILE
    last = 3

    barrier = pltpu.get_barrier_semaphore()
    for dev in ((s + 1) % 4, (s + 3) % 4):
        pl.semaphore_signal(barrier, inc=1, device_id={"section": dev}, device_id_type=MESH)

    def tile(t):
        return slice(t * TILE, (t + 1) * TILE)

    def w_copy(t):
        return pltpu.make_async_copy(weight_ref.at[0, tile(t)], w.at[tile(t)], w_sem.at[t])

    feed_copy = pltpu.make_async_copy(inputs_ref, feed, in_sem)
    cot_copy = pltpu.make_async_copy(cot_ref, grads, in_sem)

    @pl.when(s == 0)
    def _():
        feed_copy.start()

    for t in range(n_tiles):
        w_copy(t).start()

    @pl.when(s == last)
    def _():
        cot_copy.start()

    g_part[...] = jnp.zeros(g_part.shape, g_part.dtype)
    pl.semaphore_wait(barrier, 2)

    @pl.when(s == 0)
    def _():
        feed_copy.wait()

    @pl.when(s == last)
    def _():
        cot_copy.wait()

    def forward_copy(k, t):
        return pltpu.make_async_remote_copy(
            src_ref=onward.at[k, :, tile(t)],
            dst_ref=held.at[k, :, tile(t)],
            send_sem=f_send.at[k, t],
            recv_sem=f_recv.at[k, t],
            device_id={"section": (s + 1) % 4},
            device_id_type=MESH,
        )

    def backward_copy(k, t):
        return pltpu.make_async_remote_copy(
            src_ref=back.at[k, :, tile(t)],
            dst_ref=grads.at[k, :, tile(t)],
            send_sem=b_send.at[k, t],
            recv_sem=b_recv.at[k, t],
            device_id={"section": (s + 3) % 4},
            device_id_type=MESH,
        )

    def forward(k):
        @pl.when(s == 0)
        def _():
            held[k] = feed[order_ref[k]]

        for j in range(n_tiles):

            @pl.when(s > 0)
            def _():
                forward_copy(k, j).wait_recv()

            @pl.when(k == 0)
            def _():
                w_copy(j).wait()

            for t in range(n_tiles):
                z = jnp.dot(held[k, :, tile(j)], w[tile(j), tile(t)], preferred_element_type=jnp.float32)
                if j > 0:
                    z = z + total[:, tile(t)]
                if j < n_tiles - 1:
                    total[:, tile(t)] = z
                    continue
                square = z * z
                tanh_part = jnp.tanh(coef * (z + cubic * square * z))
                half = 0.5 * (1.0 + tanh_part)

                @pl.when(s < last)
                def _():
                    before = held[k, :, tile(t)].astype(jnp.float32)
                    onward[k, :, tile(t)] = (before + z * half).astype(jnp.bfloat16)
                    forward_copy(k, t).start()

                slope[k, :, tile(t)] = half + 0.5 * z * (1.0 - tanh_part * tanh_part) * coef * (
                    1.0 + 3.0 * cubic * square
                )

    def backward(k):
        for j in range(n_tiles):

            @pl.when(s < last)
            def _():
                backward_copy(k, j).wait_recv()

            g = grads[k, :, tile(j)].astype(jnp.float32)
            piece = (g * slope[k, :, tile(j)]).astype(jnp.bfloat16)
            dz[k, :, tile(j)] = piece

            @pl.when(s > 0)
            def _():
                for t in range(n_tiles):
                    value = lax.dot_general(
                        dz[k, :, tile(j)],
                        w[tile(t), tile(j)],
                        (((1,), (1,)), ((), ())),
                        preferred_element_type=jnp.float32,
                    )
                    if j > 0:
                        value = value + total[:, tile(t)]
                    if j < n_tiles - 1:
                        total[:, tile(t)] = value
                        continue
                    g = grads[k, :, tile(t)].astype(jnp.float32)
                    back[k, :, tile(t)] = (g + value).astype(jnp.bfloat16)
                    backward_copy(k, t).start()

    def turn(k):
        for part in range(8):
            block = held[k, :, part * 256 : (part + 1) * 256].T
            flipped[part * 4 : (part + 1) * 4] = block.reshape(4, 64, rows)

        lanes = pl.ds(pl.multiple_of(k * rows, rows), rows)

        def move(p, carry):
            turned_ref[p // 8, (p // 2) % 4, p % 2, :, lanes] = flipped[blocks_ref[p]]
            return carry

        lax.fori_loop(0, 32, move, 0)

    def squares():
        for z in range(4):
            for pair in range(2):
                left = turned_ref[z, pair * 2 : pair * 2 + 2].reshape(256, n_micro * rows)
                square = lax.dot_general(left, left, (((1,), (1,)), ((), ())), preferred_element_type=jnp.float32)
                for i in range(4):
                    lanes = slice(i * 64, (i + 1) * 64)
                    value = square[lanes, lanes].astype(jnp.bfloat16)
                    g_part[pair * 2 + i // 2, z // 2, z % 2, i % 2, :, 0:64] = value

    def step(k, carry):
        @pl.when(k < n_micro)
        def _():
            forward(k)

        b = k - (last - s)

        @pl.when((b >= 0) & (b < n_micro))
        def _():
            backward(b)

        @pl.when(k < n_micro)
        def _():
            turn(k)

        @pl.when(k == n_micro - 1)
        def _():
            squares()

        return carry

    lax.fori_loop(0, n_micro + last, step, 0)

    def drain(k, carry):
        @pl.when(s < last)
        def _():
            for t in range(n_tiles):
                forward_copy(k, t).wait_send()

        @pl.when(s > 0)
        def _():
            for t in range(n_tiles):
                backward_copy(k, t).wait_send()

        return carry

    lax.fori_loop(0, n_micro, drain, 0)


def relay(inputs, cotangent, weights, order, blocks_of):
    n_micro, rows, width = inputs.shape
    n_tiles = width // TILE
    bf = jnp.bfloat16
    hbm, vmem = pl.BlockSpec(memory_space=pl.ANY), pl.BlockSpec(memory_space=pltpu.VMEM)
    smem = pl.BlockSpec(memory_space=pltpu.SMEM)
    block = pltpu.VMEM((n_micro, rows, width), bf)
    dma = pltpu.SemaphoreType.DMA
    return pl.pallas_call(
        relay_kernel,
        out_shape=(
            pltpu.VMEM((4, 4, 2, 64, n_micro * rows), bf),
            block,
            pltpu.VMEM(ring_shape(GRAM[0], GRAM[1]), bf),
        ),
        in_specs=[smem, smem, hbm, hbm, hbm],
        out_specs=(vmem, vmem, vmem),
        scratch_shapes=[
            pltpu.VMEM((width, width), bf),
            block,
            block,
            pltpu.VMEM((n_micro, rows, width), jnp.float32),
            block,
            block,
            block,
            pltpu.VMEM((rows, width), jnp.float32),
            pltpu.VMEM((32, 64, rows), bf),
            dma((n_tiles,)),
            dma(()),
            dma((n_micro, n_tiles)),
            dma((n_micro, n_tiles)),
            dma((n_micro, n_tiles)),
            dma((n_micro, n_tiles)),
        ],
        compiler_params=pltpu.CompilerParams(
            collective_id=0, has_side_effects=True, vmem_limit_bytes=48 * 1024 * 1024
        ),
        name="relay",
    )(order, blocks_of, inputs, cotangent, weights)


SIZES = {"x": 4, "z": 4, "y": 2}
CHUNKS = (("yxz", 256), ("yzx", 256), ("xzy", 256), ("zxy", 256), ("xzy", 256), ("zxy", 256), ("xzy", 256), ("zxy", 256))
GRAM = ("xzy", 128)
ORDER = (8, 7, 6, 0, 7, 6, 5, 2, 1, 5, 6, 2, 7, 0, 3, 2, 7, 6, 5, 0, 4, 3, 5, 7, 0, 1, 6, 7, 0, 4, 2, 8, 6, 1, 5, 0, 6, 7, 1, 0, 4, 3, 6, 7, 2, 1, 0, 5, 8, 3, 4, 7, 1, 8, 5, 4, 2, 3, 0, 1, 6, 2, 4, 7, 3, 8, 5, 1, 0, 4, 3, 8, 6, 2, 1, 3, 4, 2, 5, 4, 7, 3, 6, 1, 5, 2, 0, 4, 3, 2, 1, 5, 4, 3)


def ring_shape(dims, wide):
    if len(dims) == 1:
        return (4, 2, 32, wide)
    if dims[1] == "y":
        return (4, 2, *(SIZES[d] for d in dims[2:]), 64, wide)
    return (4, 2, 2, *(SIZES[d] for d in dims[2:]), 64, wide)


def phase_shapes(dims, wide):
    if dims[0] == "y":
        part = (2, *(SIZES[d] for d in dims[1:]), 64, wide)
        return part, part[1:]
    part = ring_shape(dims, wide)
    return part, (6, *part[2:])


def chunk_scratch(dims, wide):
    shapes = []
    for phase in range(3):
        shapes += phase_shapes(dims[phase:], wide)
    return [pltpu.VMEM(shape, jnp.bfloat16) for shape in shapes]


def dp_kernel(*refs):
    n = len(CHUNKS)
    h_p, dz_ref, pc_ref, squares_ref = refs[:4]
    fulls, gram_ref = refs[4 : 4 + n], refs[4 + n]
    send_sem, recv_sem = refs[5 + n : 7 + n]
    scratch = refs[7 + n :]
    scratch[6 * n][...] = squares_ref[...]

    me = lax.axis_index("dp")
    my_z, my_x, my_y = me // 8, (me // 2) % 4, me % 2

    def place(z, x, y):
        return z * 8 + x * 2 + y

    up_of, down_of, far_of = (lambda v: (v + 1) % 4), (lambda v: (v + 3) % 4), (lambda v: (v + 2) % 4)
    rings = {
        "x": (my_x, place(my_z, up_of(my_x), my_y), place(my_z, down_of(my_x), my_y)),
        "z": (my_z, place(up_of(my_z), my_x, my_y), place(down_of(my_z), my_x, my_y)),
    }
    mine = {"x": my_x, "z": my_z, "y": my_y}
    mate = place(my_z, my_x, 1 - my_y)

    barrier = pltpu.get_barrier_semaphore()
    for dev in (*rings["x"][1:], *rings["z"][1:], mate):
        pl.semaphore_signal(barrier, inc=1, device_id={"dp": dev}, device_id_type=MESH)

    rows = h_p.shape[-1]
    sent = []
    f32, bf16 = jnp.float32, jnp.bfloat16

    def left_rows(first, r, half_dim, half):
        if half_dim == "y":
            return (slice(None), r, half) if first == "x" else (r, slice(None), half)
        two = slice(2 * half, 2 * half + 2)
        return (two, r) if first == "x" else (r, two)

    def flow(slot, dims, wide, offset, bufs, full):
        cols = slice(offset, offset + wide)
        counter = [0]

        def remote(src, dst, dev):
            k = counter[0]
            counter[0] += 1
            copy = pltpu.make_async_remote_copy(
                src_ref=src,
                dst_ref=dst,
                send_sem=send_sem.at[slot, k],
                recv_sem=recv_sem.at[slot, k],
                device_id={"dp": dev},
                device_id_type=MESH,
            )
            copy.start()
            sent.append(copy)
            return copy

        def product(part, index, left):
            right = dz_ref[:, :, cols].reshape(rows, wide)
            value = jnp.dot(h_p[left].reshape(256, rows), right, preferred_element_type=f32)
            part[index] = value.astype(bf16).reshape(part.shape[len(index) :])

        def no_product(part, index, left):
            pass

        make = product if full is not None else no_product

        def store(part, ring_half, total):
            if ring_half is None:
                part[...] = total.astype(bf16).reshape(part.shape)
                return
            share = part.shape[0] // 2
            if share == 1:
                part[ring_half] = total.astype(bf16).reshape(part.shape[1:])
            else:
                where = slice(share * ring_half, share * ring_half + share)
                part[where] = total.astype(bf16).reshape(share, *part.shape[1:])

        total = None
        for phase in range(3):
            d = dims[phase]
            part, landed = bufs[2 * phase], bufs[2 * phase + 1]
            then = bufs[2 * phase + 2] if phase < 2 else None
            m = mine[d]
            if d == "y":
                other = 1 - my_y
                if phase == 0:
                    first = dims[1]
                    left = lambda r, y: (slice(None), r, y) if first == "x" else (r, slice(None), y)
                    copies = []
                    for r in range(4):
                        make(part, (other, r), left(r, other))
                        copies.append(remote(part.at[other, r], landed.at[r], mate))
                    for r in range(4):
                        make(part, (my_y, r), left(r, my_y))
                    yield
                    for r in range(4):
                        copies[r].wait_recv()
                        value = part[my_y, r].astype(f32) + landed[r].astype(f32)
                        then[r] = value.astype(bf16).reshape(then.shape[1:])
                else:
                    copy = remote(part.at[other], landed, mate)
                    yield
                    copy.wait_recv()
                    total = part[my_y].astype(f32) + landed[...].astype(f32)
                    if then is not None:
                        store(then, None, total)
                continue
            up, down, far = up_of(m), down_of(m), far_of(m)
            dev_up, dev_down = rings[d][1:]
            half_dim = dims[phase + 1] if phase < 2 else None
            fill = make if phase == 0 else no_product
            left = (lambda r, h: left_rows(d, r, half_dim, h)) if phase == 0 else (lambda r, h: None)
            fill(part, (far, 0), left(far, 0))
            mp = remote(part.at[far, 0], landed.at[0], dev_up)
            fill(part, (far, 1), left(far, 1))
            mm = remote(part.at[far, 1], landed.at[1], dev_down)
            fill(part, (up, 1), left(up, 1))
            dp = remote(part.at[up, 1], landed.at[2], dev_up)
            fill(part, (down, 0), left(down, 0))
            dm = remote(part.at[down, 0], landed.at[3], dev_down)
            fill(part, (up, 0), left(up, 0))
            fill(part, (down, 1), left(down, 1))
            yield
            mp.wait_recv()
            part[up, 0] = (part[up, 0].astype(f32) + landed[0].astype(f32)).astype(bf16)
            tp = remote(part.at[up, 0], landed.at[4], dev_up)
            mm.wait_recv()
            part[down, 1] = (part[down, 1].astype(f32) + landed[1].astype(f32)).astype(bf16)
            tm = remote(part.at[down, 1], landed.at[5], dev_down)
            fill(part, (m, 0), left(m, 0))
            fill(part, (m, 1), left(m, 1))
            yield
            halves = []
            for copy in (dp, dm, tp, tm):
                copy.wait_recv()
            for half, a, b in ((0, 3, 4), (1, 2, 5)):
                value = part[m, half].astype(f32) + landed[a].astype(f32) + landed[b].astype(f32)
                if then is not None:
                    store(then, half, value)
                halves.append(value)
            if then is None:
                total = jnp.concatenate(halves, axis=0)

        if full is None:
            gram_ref[...] = total[:, 0:64] * (1.0 / 16384.0)
            return
        done = jnp.dot(pc_ref[...], total, precision=lax.Precision.HIGHEST, preferred_element_type=f32)
        own = tuple(mine[d] for d in dims)
        full[own] = done.astype(bf16)
        for phase in (2, 1, 0):
            d = dims[phase]
            lead = own[:phase]
            slab = full.at[own[: phase + 1]]
            if d == "y":
                copy = remote(slab, slab, mate)
                yield
                copy.wait_recv()
                continue
            up, down = up_of(mine[d]), down_of(mine[d])
            dev_up, dev_down = rings[d][1:]

            def half_of(r, half):
                size = 64 if phase == 2 else SIZES[dims[phase + 1]]
                return full.at[(*lead, r, pl.ds(half * (size // 2), size // 2))]

            gp = remote(slab, slab, dev_up)
            gm = remote(slab, slab, dev_down)
            yield
            gp.wait_recv()
            block = half_of(down, 0)
            fp = remote(block, block, dev_up)
            gm.wait_recv()
            block = half_of(up, 1)
            fm = remote(block, block, dev_down)
            yield
            fp.wait_recv()
            fm.wait_recv()

    pl.semaphore_wait(barrier, 5)

    flows, offset = [], 0
    for slot, (dims, wide) in enumerate((*CHUNKS, GRAM)):
        bufs = scratch[6 * slot : 6 * slot + 6]
        flows.append(flow(slot, dims, wide, offset, bufs, fulls[slot] if slot < n else None))
        offset += wide
    for slot in ORDER:
        next(flows[slot], None)
    for copy in sent:
        copy.wait_send()


def gathered_shape(dims, wide):
    return (*(SIZES[d] for d in dims), 64, wide)


def dp_part(turned, slopes, precond, squares):
    n = len(CHUNKS)
    bf = jnp.bfloat16
    vmem = pl.BlockSpec(memory_space=pltpu.VMEM)
    dma = pltpu.SemaphoreType.DMA
    scratch = []
    for dims, wide in (*CHUNKS, GRAM):
        scratch += chunk_scratch(dims, wide)
    shapes = [gathered_shape(dims, wide) for dims, wide in CHUNKS]
    *gathered, gram = pl.pallas_call(
        dp_kernel,
        out_shape=(*(pltpu.VMEM(shape, bf) for shape in shapes), pltpu.VMEM((64, 64), jnp.float32)),
        in_specs=[vmem] * 4,
        out_specs=(*(vmem for _ in shapes), vmem),
        scratch_shapes=[dma((n + 1, 26)), dma((n + 1, 26)), *scratch],
        compiler_params=pltpu.CompilerParams(
            collective_id=1, has_side_effects=True, vmem_limit_bytes=44 * 1024 * 1024
        ),
        name="dp_part",
    )(turned, slopes, precond, squares)
    return gathered, gram


def restore_kernel(owner_ref, *refs):
    n = len(CHUNKS)
    sources, gram_ref, dst_ref, gram_out, sem, gram_sem = refs[:n], *refs[n:]
    gram_copy = pltpu.make_async_copy(gram_ref, gram_out, gram_sem)
    gram_copy.start()

    def puts(b):
        o = owner_ref[b]
        at = {"z": o // 8, "x": (o // 2) % 4, "y": o % 2}
        copies, offset = [], 0
        for c, (dims, wide) in enumerate(CHUNKS):
            src = sources[c].at[tuple(at[d] for d in dims)]
            copies.append(pltpu.make_async_copy(src, dst_ref.at[b, :, pl.ds(offset, wide)], sem.at[b, c]))
            offset += wide
        return copies

    def first(b, carry):
        for copy in puts(b):
            copy.start()
        return carry

    def second(b, carry):
        for copy in puts(b):
            copy.wait()
        return carry

    lax.fori_loop(0, 32, first, 0)
    lax.fori_loop(0, 32, second, 0)
    gram_copy.wait()


def restore(gathered, gram, owner):
    n = len(CHUNKS)
    width = sum(wide for _, wide in CHUNKS)
    hbm = pl.BlockSpec(memory_space=pl.ANY)
    return pl.pallas_call(
        restore_kernel,
        out_shape=(
            jax.ShapeDtypeStruct((32, 64, width), jnp.bfloat16),
            jax.ShapeDtypeStruct(gram.shape, gram.dtype),
        ),
        in_specs=[pl.BlockSpec(memory_space=pltpu.SMEM), *[pl.BlockSpec(memory_space=pltpu.VMEM)] * (n + 1)],
        out_specs=(hbm, hbm),
        scratch_shapes=[
            pltpu.SemaphoreType.DMA((32, n)),
            pltpu.SemaphoreType.DMA(()),
        ],
        compiler_params=pltpu.CompilerParams(vmem_limit_bytes=16 * 1024 * 1024),
        name="restore",
    )(owner, *gathered, gram)


def body(inputs, cotangent, weights, preconds, order, owner):
    width = inputs.shape[2]
    n_group = owner.shape[0]
    positions = jnp.arange(n_group, dtype=jnp.int32)
    matches = (owner[None, :] == positions[:, None]).astype(jnp.int32)
    blocks_of = jnp.sum(matches * positions[None, :], axis=1)
    turned, slopes, squares = relay(inputs, cotangent, weights, order[0], blocks_of)
    gathered, gram = dp_part(turned, slopes, preconds[0, 0], squares)
    result, gram = restore(gathered, gram, owner)
    result = result.reshape(1, width, width)
    return (result, gram.reshape(1, 1, *gram.shape))


def solution(mesh):
    placed = (
        P(None, "dp", None),
        P(None, "dp", None),
        P("section", None, None),
        P("section", "dp", None, None),
        P("dp", None),
        P(),
    )
    return jax.shard_map(
        body,
        mesh=mesh,
        in_specs=placed,
        out_specs=(P("section", None, None), P("section", "dp", None, None)),
        check_vma=False,
    )
```

```python
import functools

import jax
import jax.numpy as jnp
from jax import lax
from jax.experimental import pallas as pl
from jax.experimental.pallas import tpu as pltpu
from jax.sharding import PartitionSpec as P

MESH = pl.DeviceIdType.MESH
coef = 0.7978845608028654
cubic = 0.044715


TILE = 512


def relay_kernel(
    order_ref,
    blocks_ref,
    inputs_ref,
    cot_ref,
    weight_ref,
    turned_ref,
    dz,
    g_part,
    w,
    w_t,
    feed,
    held,
    slope,
    onward,
    grads,
    back,
    total,
    flipped,
    w_sem,
    in_sem,
    f_send,
    f_recv,
    b_send,
    b_recv,
):
    s = lax.axis_index("section")
    n_micro, rows, width = held.shape
    n_tiles = width // TILE
    last = 3

    barrier = pltpu.get_barrier_semaphore()
    for dev in ((s + 1) % 4, (s + 3) % 4):
        pl.semaphore_signal(barrier, inc=1, device_id={"section": dev}, device_id_type=MESH)

    def tile(t):
        return slice(t * TILE, (t + 1) * TILE)

    def w_copy(t):
        return pltpu.make_async_copy(weight_ref.at[0, tile(t)], w.at[tile(t)], w_sem.at[t])

    feed_copy = pltpu.make_async_copy(inputs_ref, feed, in_sem)
    cot_copy = pltpu.make_async_copy(cot_ref, grads, in_sem)

    @pl.when(s == 0)
    def _():
        feed_copy.start()

    for t in range(n_tiles):
        w_copy(t).start()

    @pl.when(s == last)
    def _():
        cot_copy.start()

    g_part[...] = jnp.zeros(g_part.shape, g_part.dtype)
    pl.semaphore_wait(barrier, 2)

    @pl.when(s == 0)
    def _():
        feed_copy.wait()

    @pl.when(s == last)
    def _():
        cot_copy.wait()

    def forward_copy(k, t):
        return pltpu.make_async_remote_copy(
            src_ref=onward.at[k, :, tile(t)],
            dst_ref=held.at[k, :, tile(t)],
            send_sem=f_send.at[k, t],
            recv_sem=f_recv.at[k, t],
            device_id={"section": (s + 1) % 4},
            device_id_type=MESH,
        )

    def backward_copy(k, t):
        return pltpu.make_async_remote_copy(
            src_ref=back.at[k, :, tile(t)],
            dst_ref=grads.at[k, :, tile(t)],
            send_sem=b_send.at[k, t],
            recv_sem=b_recv.at[k, t],
            device_id={"section": (s + 3) % 4},
            device_id_type=MESH,
        )

    def turn_weight():
        def strip(r, carry):
            at = pl.ds(pl.multiple_of(r * 256, 256), 256)
            for c in range(width // 256):
                cols = slice(c * 256, (c + 1) * 256)
                w_t[cols, at] = w[at, cols].T
            return carry

        lax.fori_loop(0, width // 256, strip, 0)

    def forward(k):
        @pl.when(s == 0)
        def _():
            held[k] = feed[order_ref[k]]

        for j in range(n_tiles):

            @pl.when(s > 0)
            def _():
                forward_copy(k, j).wait_recv()

            @pl.when((k == 0) & (s < 2))
            def _():
                w_copy(j).wait()

            for t in range(n_tiles):
                z = jnp.dot(held[k, :, tile(j)], w[tile(j), tile(t)], preferred_element_type=jnp.float32)
                if j > 0:
                    z = z + total[:, tile(t)]
                if j < n_tiles - 1:
                    total[:, tile(t)] = z
                    continue
                square = z * z
                tanh_part = jnp.tanh(coef * (z + cubic * square * z))
                half = 0.5 * (1.0 + tanh_part)
                before = held[k, :, tile(t)].astype(jnp.float32)
                onward[k, :, tile(t)] = (before + z * half).astype(jnp.bfloat16)

                @pl.when(s < last)
                def _():
                    forward_copy(k, t).start()

                slope[k, :, tile(t)] = half + 0.5 * z * (1.0 - tanh_part * tanh_part) * coef * (
                    1.0 + 3.0 * cubic * square
                )

    def backward(k):
        for j in range(n_tiles):

            @pl.when(s < last)
            def _():
                backward_copy(k, j).wait_recv()

            g = grads[k, :, tile(j)].astype(jnp.float32)
            piece = (g * slope[k, :, tile(j)]).astype(jnp.bfloat16)
            dz[k, :, tile(j)] = piece

            @pl.when(s > 0)
            def _():
                for t in range(n_tiles):
                    value = jnp.dot(
                        dz[k, :, tile(j)], w_t[tile(j), tile(t)], preferred_element_type=jnp.float32
                    )
                    if j > 0:
                        value = value + total[:, tile(t)]
                    if j < n_tiles - 1:
                        total[:, tile(t)] = value
                        continue
                    g = grads[k, :, tile(t)].astype(jnp.float32)
                    back[k, :, tile(t)] = (g + value).astype(jnp.bfloat16)
                    backward_copy(k, t).start()

    def turn(k):
        for part in range(8):
            block = held[k, :, part * 256 : (part + 1) * 256].T
            flipped[part * 4 : (part + 1) * 4] = block.reshape(4, 64, rows)

        lanes = pl.ds(pl.multiple_of(k * rows, rows), rows)

        def move(p, carry):
            turned_ref[p // 8, (p // 2) % 4, p % 2, :, lanes] = flipped[blocks_ref[p]]
            return carry

        lax.fori_loop(0, 32, move, 0)

    def squares():
        for z in range(4):
            for pair in range(2):
                left = turned_ref[z, pair * 2 : pair * 2 + 2].reshape(256, n_micro * rows)
                square = lax.dot_general(left, left, (((1,), (1,)), ((), ())), preferred_element_type=jnp.float32)
                for i in range(4):
                    lanes = slice(i * 64, (i + 1) * 64)
                    value = square[lanes, lanes].astype(jnp.bfloat16)
                    g_part[pair * 2 + i // 2, z // 2, z % 2, i % 2, :, 0:64] = value

    def step(k, carry):
        @pl.when(k < n_micro)
        def _():
            forward(k)

        @pl.when((k == n_micro - 1) & (s == 1))
        def _():
            turn_weight()

        b = k - jnp.where(s < 2, last, last - s)

        @pl.when((b >= 0) & (b < n_micro))
        def _():
            backward(b)

        @pl.when(k < n_micro)
        def _():
            turn(k)

        @pl.when(k == n_micro - 1)
        def _():
            squares()

        return carry

    @pl.when(s >= 2)
    def _():
        for t in range(n_tiles):
            w_copy(t).wait()
        turn_weight()

    lax.fori_loop(0, n_micro + last, step, 0)

    def drain(k, carry):
        @pl.when(s < last)
        def _():
            for t in range(n_tiles):
                forward_copy(k, t).wait_send()

        @pl.when(s > 0)
        def _():
            for t in range(n_tiles):
                backward_copy(k, t).wait_send()

        return carry

    lax.fori_loop(0, n_micro, drain, 0)


def relay(inputs, cotangent, weights, order, blocks_of):
    n_micro, rows, width = inputs.shape
    n_tiles = width // TILE
    bf = jnp.bfloat16
    hbm, vmem = pl.BlockSpec(memory_space=pl.ANY), pl.BlockSpec(memory_space=pltpu.VMEM)
    smem = pl.BlockSpec(memory_space=pltpu.SMEM)
    block = pltpu.VMEM((n_micro, rows, width), bf)
    dma = pltpu.SemaphoreType.DMA
    return pl.pallas_call(
        relay_kernel,
        out_shape=(
            pltpu.VMEM((4, 4, 2, 64, n_micro * rows), bf),
            block,
            pltpu.VMEM(ring_shape(GRAM[0], GRAM[1]), bf),
        ),
        in_specs=[smem, smem, hbm, hbm, hbm],
        out_specs=(vmem, vmem, vmem),
        scratch_shapes=[
            pltpu.VMEM((width, width), bf),
            pltpu.VMEM((width, width), bf),
            block,
            block,
            pltpu.VMEM((n_micro, rows, width), jnp.float32),
            block,
            block,
            block,
            pltpu.VMEM((rows, width), jnp.float32),
            pltpu.VMEM((32, 64, rows), bf),
            dma((n_tiles,)),
            dma(()),
            dma((n_micro, n_tiles)),
            dma((n_micro, n_tiles)),
            dma((n_micro, n_tiles)),
            dma((n_micro, n_tiles)),
        ],
        compiler_params=pltpu.CompilerParams(
            collective_id=0, has_side_effects=True, vmem_limit_bytes=57 * 1024 * 1024
        ),
        name="relay",
    )(order, blocks_of, inputs, cotangent, weights)


SIZES = {"x": 4, "z": 4, "y": 2}
CHUNKS = (("yxz", 256), ("yzx", 256), ("xzy", 256), ("zxy", 256), ("xzy", 256), ("zxy", 256), ("xzy", 256), ("zxy", 256))
GRAM = ("xzy", 128)
ORDER = (8, 7, 6, 0, 7, 6, 5, 2, 1, 5, 6, 2, 7, 0, 3, 2, 7, 6, 5, 0, 4, 3, 5, 7, 0, 1, 6, 7, 0, 4, 2, 8, 6, 1, 5, 0, 6, 7, 1, 0, 4, 3, 6, 7, 2, 1, 0, 5, 8, 3, 4, 7, 1, 8, 5, 4, 2, 3, 0, 1, 6, 2, 4, 7, 3, 8, 5, 1, 0, 4, 3, 8, 6, 2, 1, 3, 4, 2, 5, 4, 7, 3, 6, 1, 5, 2, 0, 4, 3, 2, 1, 5, 4, 3)


def ring_shape(dims, wide):
    if len(dims) == 1:
        return (4, 2, 32, wide)
    if dims[1] == "y":
        return (4, 2, *(SIZES[d] for d in dims[2:]), 64, wide)
    return (4, 2, 2, *(SIZES[d] for d in dims[2:]), 64, wide)


def phase_shapes(dims, wide):
    if dims[0] == "y":
        part = (2, *(SIZES[d] for d in dims[1:]), 64, wide)
        return part, part[1:]
    part = ring_shape(dims, wide)
    return part, (6, *part[2:])


def chunk_scratch(dims, wide):
    shapes = []
    for phase in range(3):
        shapes += phase_shapes(dims[phase:], wide)
    return [pltpu.VMEM(shape, jnp.bfloat16) for shape in shapes]


def dp_kernel(*refs):
    n = len(CHUNKS)
    h_p, dz_ref, pc_ref, squares_ref = refs[:4]
    fulls, gram_ref = refs[4 : 4 + n], refs[4 + n]
    send_sem, recv_sem = refs[5 + n : 7 + n]
    scratch = refs[7 + n :]
    scratch[6 * n][...] = squares_ref[...]

    me = lax.axis_index("dp")
    my_z, my_x, my_y = me // 8, (me // 2) % 4, me % 2

    def place(z, x, y):
        return z * 8 + x * 2 + y

    up_of, down_of, far_of = (lambda v: (v + 1) % 4), (lambda v: (v + 3) % 4), (lambda v: (v + 2) % 4)
    rings = {
        "x": (my_x, place(my_z, up_of(my_x), my_y), place(my_z, down_of(my_x), my_y)),
        "z": (my_z, place(up_of(my_z), my_x, my_y), place(down_of(my_z), my_x, my_y)),
    }
    mine = {"x": my_x, "z": my_z, "y": my_y}
    mate = place(my_z, my_x, 1 - my_y)

    barrier = pltpu.get_barrier_semaphore()
    for dev in (*rings["x"][1:], *rings["z"][1:], mate):
        pl.semaphore_signal(barrier, inc=1, device_id={"dp": dev}, device_id_type=MESH)

    rows = h_p.shape[-1]
    sent = []
    f32, bf16 = jnp.float32, jnp.bfloat16

    def left_rows(first, r, half_dim, half):
        if half_dim == "y":
            return (slice(None), r, half) if first == "x" else (r, slice(None), half)
        two = slice(2 * half, 2 * half + 2)
        return (two, r) if first == "x" else (r, two)

    def flow(slot, dims, wide, offset, bufs, full):
        cols = slice(offset, offset + wide)
        counter = [0]

        def remote(src, dst, dev):
            k = counter[0]
            counter[0] += 1
            copy = pltpu.make_async_remote_copy(
                src_ref=src,
                dst_ref=dst,
                send_sem=send_sem.at[slot, k],
                recv_sem=recv_sem.at[slot, k],
                device_id={"dp": dev},
                device_id_type=MESH,
            )
            copy.start()
            sent.append(copy)
            return copy

        def product(part, index, left):
            right = dz_ref[:, :, cols].reshape(rows, wide)
            value = jnp.dot(h_p[left].reshape(256, rows), right, preferred_element_type=f32)
            part[index] = value.astype(bf16).reshape(part.shape[len(index) :])

        def no_product(part, index, left):
            pass

        make = product if full is not None else no_product

        def store(part, ring_half, total):
            if ring_half is None:
                part[...] = total.astype(bf16).reshape(part.shape)
                return
            share = part.shape[0] // 2
            if share == 1:
                part[ring_half] = total.astype(bf16).reshape(part.shape[1:])
            else:
                where = slice(share * ring_half, share * ring_half + share)
                part[where] = total.astype(bf16).reshape(share, *part.shape[1:])

        total = None
        for phase in range(3):
            d = dims[phase]
            part, landed = bufs[2 * phase], bufs[2 * phase + 1]
            then = bufs[2 * phase + 2] if phase < 2 else None
            m = mine[d]
            if d == "y":
                other = 1 - my_y
                if phase == 0:
                    first = dims[1]
                    left = lambda r, y: (slice(None), r, y) if first == "x" else (r, slice(None), y)
                    copies = []
                    for r in range(4):
                        make(part, (other, r), left(r, other))
                        copies.append(remote(part.at[other, r], landed.at[r], mate))
                    for r in range(4):
                        make(part, (my_y, r), left(r, my_y))
                    yield
                    for r in range(4):
                        copies[r].wait_recv()
                        value = part[my_y, r].astype(f32) + landed[r].astype(f32)
                        then[r] = value.astype(bf16).reshape(then.shape[1:])
                else:
                    copy = remote(part.at[other], landed, mate)
                    yield
                    copy.wait_recv()
                    total = part[my_y].astype(f32) + landed[...].astype(f32)
                    if then is not None:
                        store(then, None, total)
                continue
            up, down, far = up_of(m), down_of(m), far_of(m)
            dev_up, dev_down = rings[d][1:]
            half_dim = dims[phase + 1] if phase < 2 else None
            fill = make if phase == 0 else no_product
            left = (lambda r, h: left_rows(d, r, half_dim, h)) if phase == 0 else (lambda r, h: None)
            fill(part, (far, 0), left(far, 0))
            mp = remote(part.at[far, 0], landed.at[0], dev_up)
            fill(part, (far, 1), left(far, 1))
            mm = remote(part.at[far, 1], landed.at[1], dev_down)
            fill(part, (up, 1), left(up, 1))
            dp = remote(part.at[up, 1], landed.at[2], dev_up)
            fill(part, (down, 0), left(down, 0))
            dm = remote(part.at[down, 0], landed.at[3], dev_down)
            fill(part, (up, 0), left(up, 0))
            fill(part, (down, 1), left(down, 1))
            yield
            mp.wait_recv()
            part[up, 0] = (part[up, 0].astype(f32) + landed[0].astype(f32)).astype(bf16)
            tp = remote(part.at[up, 0], landed.at[4], dev_up)
            mm.wait_recv()
            part[down, 1] = (part[down, 1].astype(f32) + landed[1].astype(f32)).astype(bf16)
            tm = remote(part.at[down, 1], landed.at[5], dev_down)
            fill(part, (m, 0), left(m, 0))
            fill(part, (m, 1), left(m, 1))
            yield
            halves = []
            for copy in (dp, dm, tp, tm):
                copy.wait_recv()
            for half, a, b in ((0, 3, 4), (1, 2, 5)):
                value = part[m, half].astype(f32) + landed[a].astype(f32) + landed[b].astype(f32)
                if then is not None:
                    store(then, half, value)
                halves.append(value)
            if then is None:
                total = jnp.concatenate(halves, axis=0)

        if full is None:
            gram_ref[...] = total[:, 0:64] * (1.0 / 16384.0)
            return
        done = jnp.dot(pc_ref[...], total, precision=lax.Precision.HIGHEST, preferred_element_type=f32)
        own = tuple(mine[d] for d in dims)
        full[own] = done.astype(bf16)
        for phase in (2, 1, 0):
            d = dims[phase]
            lead = own[:phase]
            slab = full.at[own[: phase + 1]]
            if d == "y":
                copy = remote(slab, slab, mate)
                yield
                copy.wait_recv()
                continue
            up, down = up_of(mine[d]), down_of(mine[d])
            dev_up, dev_down = rings[d][1:]

            def half_of(r, half):
                size = 64 if phase == 2 else SIZES[dims[phase + 1]]
                return full.at[(*lead, r, pl.ds(half * (size // 2), size // 2))]

            gp = remote(slab, slab, dev_up)
            gm = remote(slab, slab, dev_down)
            yield
            gp.wait_recv()
            block = half_of(down, 0)
            fp = remote(block, block, dev_up)
            gm.wait_recv()
            block = half_of(up, 1)
            fm = remote(block, block, dev_down)
            yield
            fp.wait_recv()
            fm.wait_recv()

    pl.semaphore_wait(barrier, 5)

    flows, offset = [], 0
    for slot, (dims, wide) in enumerate((*CHUNKS, GRAM)):
        bufs = scratch[6 * slot : 6 * slot + 6]
        flows.append(flow(slot, dims, wide, offset, bufs, fulls[slot] if slot < n else None))
        offset += wide
    for slot in ORDER:
        next(flows[slot], None)
    for copy in sent:
        copy.wait_send()


def gathered_shape(dims, wide):
    return (*(SIZES[d] for d in dims), 64, wide)


def dp_part(turned, slopes, precond, squares):
    n = len(CHUNKS)
    bf = jnp.bfloat16
    vmem = pl.BlockSpec(memory_space=pltpu.VMEM)
    dma = pltpu.SemaphoreType.DMA
    scratch = []
    for dims, wide in (*CHUNKS, GRAM):
        scratch += chunk_scratch(dims, wide)
    shapes = [gathered_shape(dims, wide) for dims, wide in CHUNKS]
    *gathered, gram = pl.pallas_call(
        dp_kernel,
        out_shape=(*(pltpu.VMEM(shape, bf) for shape in shapes), pltpu.VMEM((64, 64), jnp.float32)),
        in_specs=[vmem] * 4,
        out_specs=(*(vmem for _ in shapes), vmem),
        scratch_shapes=[dma((n + 1, 26)), dma((n + 1, 26)), *scratch],
        compiler_params=pltpu.CompilerParams(
            collective_id=1, has_side_effects=True, vmem_limit_bytes=32 * 1024 * 1024
        ),
        name="dp_part",
    )(turned, slopes, precond, squares)
    return gathered, gram


def restore_kernel(owner_ref, *refs):
    n = len(CHUNKS)
    sources, gram_ref, dst_ref, gram_out, sem, gram_sem = refs[:n], *refs[n:]
    gram_copy = pltpu.make_async_copy(gram_ref, gram_out, gram_sem)
    gram_copy.start()

    def puts(b):
        o = owner_ref[b]
        at = {"z": o // 8, "x": (o // 2) % 4, "y": o % 2}
        copies, offset = [], 0
        for c, (dims, wide) in enumerate(CHUNKS):
            src = sources[c].at[tuple(at[d] for d in dims)]
            copies.append(pltpu.make_async_copy(src, dst_ref.at[b, :, pl.ds(offset, wide)], sem.at[b, c]))
            offset += wide
        return copies

    def first(b, carry):
        for copy in puts(b):
            copy.start()
        return carry

    def second(b, carry):
        for copy in puts(b):
            copy.wait()
        return carry

    lax.fori_loop(0, 32, first, 0)
    lax.fori_loop(0, 32, second, 0)
    gram_copy.wait()


def restore(gathered, gram, owner):
    n = len(CHUNKS)
    width = sum(wide for _, wide in CHUNKS)
    hbm = pl.BlockSpec(memory_space=pl.ANY)
    return pl.pallas_call(
        restore_kernel,
        out_shape=(
            jax.ShapeDtypeStruct((32, 64, width), jnp.bfloat16),
            jax.ShapeDtypeStruct(gram.shape, gram.dtype),
        ),
        in_specs=[pl.BlockSpec(memory_space=pltpu.SMEM), *[pl.BlockSpec(memory_space=pltpu.VMEM)] * (n + 1)],
        out_specs=(hbm, hbm),
        scratch_shapes=[
            pltpu.SemaphoreType.DMA((32, n)),
            pltpu.SemaphoreType.DMA(()),
        ],
        compiler_params=pltpu.CompilerParams(vmem_limit_bytes=16 * 1024 * 1024),
        name="restore",
    )(owner, *gathered, gram)


def body(inputs, cotangent, weights, preconds, order, owner):
    width = inputs.shape[2]
    n_group = owner.shape[0]
    positions = jnp.arange(n_group, dtype=jnp.int32)
    matches = (owner[None, :] == positions[:, None]).astype(jnp.int32)
    blocks_of = jnp.sum(matches * positions[None, :], axis=1)
    turned, slopes, squares = relay(inputs, cotangent, weights, order[0], blocks_of)
    gathered, gram = dp_part(turned, slopes, preconds[0, 0], squares)
    result, gram = restore(gathered, gram, owner)
    result = result.reshape(1, width, width)
    return (result, gram.reshape(1, 1, *gram.shape))


def solution(mesh):
    placed = (
        P(None, "dp", None),
        P(None, "dp", None),
        P("section", None, None),
        P("section", "dp", None, None),
        P("dp", None),
        P(),
    )
    return jax.shard_map(
        body,
        mesh=mesh,
        in_specs=placed,
        out_specs=(P("section", None, None), P("section", "dp", None, None)),
        check_vma=False,
    )
```

```python
import functools

import jax
import jax.numpy as jnp
from jax import lax
from jax.experimental import pallas as pl
from jax.experimental.pallas import tpu as pltpu
from jax.sharding import PartitionSpec as P

MESH = pl.DeviceIdType.MESH
coef = 0.7978845608028654
cubic = 0.044715


TILE = 512


def relay_kernel(
    order_ref,
    owner_ref,
    inputs_ref,
    cot_ref,
    weight_ref,
    turned_ref,
    dz,
    g_part,
    w,
    w_t,
    feed,
    held,
    slope,
    onward,
    grads,
    back,
    total,
    flipped,
    blocks_ref,
    w_sem,
    in_sem,
    f_send,
    f_recv,
    b_send,
    b_recv,
):
    s = lax.axis_index("section")
    n_micro, rows, width = held.shape
    n_tiles = width // TILE
    last = 3

    barrier = pltpu.get_barrier_semaphore()
    for dev in ((s + 1) % 4, (s + 3) % 4):
        pl.semaphore_signal(barrier, inc=1, device_id={"section": dev}, device_id_type=MESH)

    def find(p, carry):
        block = jnp.int32(0)
        for b in range(32):
            block = jnp.where(owner_ref[b] == p, jnp.int32(b), block)
        blocks_ref[p] = block
        return carry

    def tile(t):
        return slice(t * TILE, (t + 1) * TILE)

    def w_copy(t):
        return pltpu.make_async_copy(weight_ref.at[0, tile(t)], w.at[tile(t)], w_sem.at[t])

    feed_copy = pltpu.make_async_copy(inputs_ref, feed, in_sem)
    cot_copy = pltpu.make_async_copy(cot_ref, grads, in_sem)

    @pl.when(s == 0)
    def _():
        feed_copy.start()

    for t in range(n_tiles):
        w_copy(t).start()

    @pl.when(s == last)
    def _():
        cot_copy.start()

    g_part[...] = jnp.zeros(g_part.shape, g_part.dtype)
    lax.fori_loop(0, 32, find, 0)
    pl.semaphore_wait(barrier, 2)

    @pl.when(s == 0)
    def _():
        feed_copy.wait()

    @pl.when(s == last)
    def _():
        cot_copy.wait()

    def forward_copy(k, t):
        return pltpu.make_async_remote_copy(
            src_ref=onward.at[k, :, tile(t)],
            dst_ref=held.at[k, :, tile(t)],
            send_sem=f_send.at[k, t],
            recv_sem=f_recv.at[k, t],
            device_id={"section": (s + 1) % 4},
            device_id_type=MESH,
        )

    def backward_copy(k, t):
        return pltpu.make_async_remote_copy(
            src_ref=back.at[k, :, tile(t)],
            dst_ref=grads.at[k, :, tile(t)],
            send_sem=b_send.at[k, t],
            recv_sem=b_recv.at[k, t],
            device_id={"section": (s + 3) % 4},
            device_id_type=MESH,
        )

    def turn_weight():
        def strip(r, carry):
            at = pl.ds(pl.multiple_of(r * 256, 256), 256)
            for c in range(width // 256):
                cols = slice(c * 256, (c + 1) * 256)
                w_t[cols, at] = w[at, cols].T
            return carry

        lax.fori_loop(0, width // 256, strip, 0)

    def forward(k):
        @pl.when(s == 0)
        def _():
            held[k] = feed[order_ref[k // 2] * 2 + k % 2]

        for j in range(n_tiles):

            @pl.when(s > 0)
            def _():
                forward_copy(k, j).wait_recv()

            @pl.when((k == 0) & (s < 2))
            def _():
                w_copy(j).wait()

            for t in range(n_tiles):
                z = jnp.dot(held[k, :, tile(j)], w[tile(j), tile(t)], preferred_element_type=jnp.float32)
                if j > 0:
                    z = z + total[:, tile(t)]
                if j < n_tiles - 1:
                    total[:, tile(t)] = z
                    continue
                square = z * z
                tanh_part = jnp.tanh(coef * (z + cubic * square * z))
                half = 0.5 * (1.0 + tanh_part)
                before = held[k, :, tile(t)].astype(jnp.float32)
                onward[k, :, tile(t)] = (before + z * half).astype(jnp.bfloat16)

                @pl.when(s < last)
                def _():
                    forward_copy(k, t).start()

                slope[k, :, tile(t)] = half + 0.5 * z * (1.0 - tanh_part * tanh_part) * coef * (
                    1.0 + 3.0 * cubic * square
                )

    def backward(k):
        for j in range(n_tiles):

            @pl.when(s < last)
            def _():
                backward_copy(k, j).wait_recv()

            g = grads[k, :, tile(j)].astype(jnp.float32)
            piece = (g * slope[k, :, tile(j)]).astype(jnp.bfloat16)
            dz[k, :, tile(j)] = piece

            @pl.when(s > 0)
            def _():
                for t in range(n_tiles):
                    value = jnp.dot(
                        dz[k, :, tile(j)], w_t[tile(j), tile(t)], preferred_element_type=jnp.float32
                    )
                    if j > 0:
                        value = value + total[:, tile(t)]
                    if j < n_tiles - 1:
                        total[:, tile(t)] = value
                        continue
                    g = grads[k, :, tile(t)].astype(jnp.float32)
                    back[k, :, tile(t)] = (g + value).astype(jnp.bfloat16)
                    backward_copy(k, t).start()

    def turn(m):
        for part in range(8):
            pair = held[pl.ds(m * 2, 2), :, part * 256 : (part + 1) * 256]
            flipped[part * 4 : (part + 1) * 4] = pair.reshape(2 * rows, 256).T.reshape(4, 64, 2 * rows)

        lanes = pl.ds(pl.multiple_of(m * 2 * rows, 2 * rows), 2 * rows)

        def move(p, carry):
            turned_ref[p // 8, (p // 2) % 4, p % 2, :, lanes] = flipped[blocks_ref[p]]
            return carry

        lax.fori_loop(0, 32, move, 0)

    def squares():
        for z in range(4):
            for pair in range(2):
                left = turned_ref[z, pair * 2 : pair * 2 + 2].reshape(256, n_micro * rows)
                square = lax.dot_general(left, left, (((1,), (1,)), ((), ())), preferred_element_type=jnp.float32)
                for i in range(4):
                    lanes = slice(i * 64, (i + 1) * 64)
                    value = square[lanes, lanes].astype(jnp.bfloat16)
                    g_part[pair * 2 + i // 2, z // 2, z % 2, i % 2, :, 0:64] = value

    def step(k, carry):
        @pl.when(k < n_micro)
        def _():
            forward(k)

        @pl.when((k == n_micro - 1) & (s == 1))
        def _():
            turn_weight()

        b = k - jnp.where(s < 2, n_micro - 1, (last - s) * 2)

        @pl.when((b >= 0) & (b < n_micro))
        def _():
            backward(b)

        @pl.when((k < n_micro) & (k % 2 == 1))
        def _():
            turn(k // 2)

        @pl.when(k == n_micro - 1)
        def _():
            squares()

        return carry

    @pl.when(s >= 2)
    def _():
        for t in range(n_tiles):
            w_copy(t).wait()
        turn_weight()

    lax.fori_loop(0, 2 * n_micro - 1, step, 0)

    def drain(k, carry):
        @pl.when(s < last)
        def _():
            for t in range(n_tiles):
                forward_copy(k, t).wait_send()

        @pl.when(s > 0)
        def _():
            for t in range(n_tiles):
                backward_copy(k, t).wait_send()

        return carry

    lax.fori_loop(0, n_micro, drain, 0)


def relay(inputs, cotangent, weights, order, owner):
    n_micro, rows, width = inputs.shape[0] * 2, inputs.shape[1] // 2, inputs.shape[2]
    inputs, cotangent = (array.reshape(n_micro, rows, width) for array in (inputs, cotangent))
    n_tiles = width // TILE
    bf = jnp.bfloat16
    hbm, vmem = pl.BlockSpec(memory_space=pl.ANY), pl.BlockSpec(memory_space=pltpu.VMEM)
    smem = pl.BlockSpec(memory_space=pltpu.SMEM)
    block = pltpu.VMEM((n_micro, rows, width), bf)
    dma = pltpu.SemaphoreType.DMA
    return pl.pallas_call(
        relay_kernel,
        out_shape=(
            pltpu.VMEM((4, 4, 2, 64, n_micro * rows), bf),
            block,
            pltpu.VMEM(ring_shape(GRAM[0], GRAM[1]), bf),
        ),
        in_specs=[smem, smem, hbm, hbm, hbm],
        out_specs=(vmem, vmem, vmem),
        scratch_shapes=[
            pltpu.VMEM((width, width), bf),
            pltpu.VMEM((width, width), bf),
            block,
            block,
            pltpu.VMEM((n_micro, rows, width), jnp.float32),
            block,
            block,
            block,
            pltpu.VMEM((rows, width), jnp.float32),
            pltpu.VMEM((32, 64, 2 * rows), bf),
            pltpu.SMEM((32,), jnp.int32),
            dma((n_tiles,)),
            dma(()),
            dma((n_micro, n_tiles)),
            dma((n_micro, n_tiles)),
            dma((n_micro, n_tiles)),
            dma((n_micro, n_tiles)),
        ],
        compiler_params=pltpu.CompilerParams(
            collective_id=0, has_side_effects=True, vmem_limit_bytes=57 * 1024 * 1024
        ),
        name="relay",
    )(order, owner, inputs, cotangent, weights)


SIZES = {"x": 4, "z": 4, "y": 2}
CHUNKS = (("yxz", 256), ("yzx", 256), ("xzy", 256), ("zxy", 256), ("xzy", 256), ("zxy", 256), ("xzy", 256), ("zxy", 256))
GRAM = ("xzy", 128)
ORDER = (8, 7, 6, 0, 7, 6, 5, 2, 1, 5, 6, 2, 7, 0, 3, 2, 7, 6, 5, 0, 4, 3, 5, 7, 0, 1, 6, 7, 0, 4, 2, 8, 6, 1, 5, 0, 6, 7, 1, 0, 4, 3, 6, 7, 2, 1, 0, 5, 8, 3, 4, 7, 1, 8, 5, 4, 2, 3, 0, 1, 6, 2, 4, 7, 3, 8, 5, 1, 0, 4, 3, 8, 6, 2, 1, 3, 4, 2, 5, 4, 7, 3, 6, 1, 5, 2, 0, 4, 3, 2, 1, 5, 4, 3)


def ring_shape(dims, wide):
    if len(dims) == 1:
        return (4, 2, 32, wide)
    if dims[1] == "y":
        return (4, 2, *(SIZES[d] for d in dims[2:]), 64, wide)
    return (4, 2, 2, *(SIZES[d] for d in dims[2:]), 64, wide)


def phase_shapes(dims, wide):
    if dims[0] == "y":
        part = (2, *(SIZES[d] for d in dims[1:]), 64, wide)
        return part, part[1:]
    part = ring_shape(dims, wide)
    return part, (6, *part[2:])


def chunk_scratch(dims, wide):
    shapes = []
    for phase in range(3):
        shapes += phase_shapes(dims[phase:], wide)
    return [pltpu.VMEM(shape, jnp.bfloat16) for shape in shapes]


def dp_kernel(*refs):
    n = len(CHUNKS)
    h_p, dz_ref, pc_ref, squares_ref = refs[:4]
    fulls, gram_ref = refs[4 : 4 + n], refs[4 + n]
    send_sem, recv_sem = refs[5 + n : 7 + n]
    scratch = refs[7 + n :]
    scratch[6 * n][...] = squares_ref[...]

    me = lax.axis_index("dp")
    my_z, my_x, my_y = me // 8, (me // 2) % 4, me % 2

    def place(z, x, y):
        return z * 8 + x * 2 + y

    up_of, down_of, far_of = (lambda v: (v + 1) % 4), (lambda v: (v + 3) % 4), (lambda v: (v + 2) % 4)
    rings = {
        "x": (my_x, place(my_z, up_of(my_x), my_y), place(my_z, down_of(my_x), my_y)),
        "z": (my_z, place(up_of(my_z), my_x, my_y), place(down_of(my_z), my_x, my_y)),
    }
    mine = {"x": my_x, "z": my_z, "y": my_y}
    mate = place(my_z, my_x, 1 - my_y)

    barrier = pltpu.get_barrier_semaphore()
    for dev in (*rings["x"][1:], *rings["z"][1:], mate):
        pl.semaphore_signal(barrier, inc=1, device_id={"dp": dev}, device_id_type=MESH)

    rows = h_p.shape[-1]
    sent = []
    f32, bf16 = jnp.float32, jnp.bfloat16

    def left_rows(first, r, half_dim, half):
        if half_dim == "y":
            return (slice(None), r, half) if first == "x" else (r, slice(None), half)
        two = slice(2 * half, 2 * half + 2)
        return (two, r) if first == "x" else (r, two)

    def flow(slot, dims, wide, offset, bufs, full):
        cols = slice(offset, offset + wide)
        counter = [0]

        def remote(src, dst, dev):
            k = counter[0]
            counter[0] += 1
            copy = pltpu.make_async_remote_copy(
                src_ref=src,
                dst_ref=dst,
                send_sem=send_sem.at[slot, k],
                recv_sem=recv_sem.at[slot, k],
                device_id={"dp": dev},
                device_id_type=MESH,
            )
            copy.start()
            sent.append(copy)
            return copy

        def product(part, index, left):
            right = dz_ref[:, :, cols].reshape(rows, wide)
            value = jnp.dot(h_p[left].reshape(256, rows), right, preferred_element_type=f32)
            part[index] = value.astype(bf16).reshape(part.shape[len(index) :])

        def no_product(part, index, left):
            pass

        make = product if full is not None else no_product

        def store(part, ring_half, total):
            if ring_half is None:
                part[...] = total.astype(bf16).reshape(part.shape)
                return
            share = part.shape[0] // 2
            if share == 1:
                part[ring_half] = total.astype(bf16).reshape(part.shape[1:])
            else:
                where = slice(share * ring_half, share * ring_half + share)
                part[where] = total.astype(bf16).reshape(share, *part.shape[1:])

        total = None
        for phase in range(3):
            d = dims[phase]
            part, landed = bufs[2 * phase], bufs[2 * phase + 1]
            then = bufs[2 * phase + 2] if phase < 2 else None
            m = mine[d]
            if d == "y":
                other = 1 - my_y
                if phase == 0:
                    first = dims[1]
                    left = lambda r, y: (slice(None), r, y) if first == "x" else (r, slice(None), y)
                    copies = []
                    for r in range(4):
                        make(part, (other, r), left(r, other))
                        copies.append(remote(part.at[other, r], landed.at[r], mate))
                    for r in range(4):
                        make(part, (my_y, r), left(r, my_y))
                    yield
                    for r in range(4):
                        copies[r].wait_recv()
                        value = part[my_y, r].astype(f32) + landed[r].astype(f32)
                        then[r] = value.astype(bf16).reshape(then.shape[1:])
                else:
                    copy = remote(part.at[other], landed, mate)
                    yield
                    copy.wait_recv()
                    total = part[my_y].astype(f32) + landed[...].astype(f32)
                    if then is not None:
                        store(then, None, total)
                continue
            up, down, far = up_of(m), down_of(m), far_of(m)
            dev_up, dev_down = rings[d][1:]
            half_dim = dims[phase + 1] if phase < 2 else None
            fill = make if phase == 0 else no_product
            left = (lambda r, h: left_rows(d, r, half_dim, h)) if phase == 0 else (lambda r, h: None)
            fill(part, (far, 0), left(far, 0))
            mp = remote(part.at[far, 0], landed.at[0], dev_up)
            fill(part, (far, 1), left(far, 1))
            mm = remote(part.at[far, 1], landed.at[1], dev_down)
            fill(part, (up, 1), left(up, 1))
            dp = remote(part.at[up, 1], landed.at[2], dev_up)
            fill(part, (down, 0), left(down, 0))
            dm = remote(part.at[down, 0], landed.at[3], dev_down)
            fill(part, (up, 0), left(up, 0))
            fill(part, (down, 1), left(down, 1))
            yield
            mp.wait_recv()
            part[up, 0] = (part[up, 0].astype(f32) + landed[0].astype(f32)).astype(bf16)
            tp = remote(part.at[up, 0], landed.at[4], dev_up)
            mm.wait_recv()
            part[down, 1] = (part[down, 1].astype(f32) + landed[1].astype(f32)).astype(bf16)
            tm = remote(part.at[down, 1], landed.at[5], dev_down)
            fill(part, (m, 0), left(m, 0))
            fill(part, (m, 1), left(m, 1))
            yield
            halves = []
            for copy in (dp, dm, tp, tm):
                copy.wait_recv()
            for half, a, b in ((0, 3, 4), (1, 2, 5)):
                value = part[m, half].astype(f32) + landed[a].astype(f32) + landed[b].astype(f32)
                if then is not None:
                    store(then, half, value)
                halves.append(value)
            if then is None:
                total = jnp.concatenate(halves, axis=0)

        if full is None:
            gram_ref[...] = total[:, 0:64] * (1.0 / 16384.0)
            return
        done = jnp.dot(pc_ref[...], total, precision=lax.Precision.HIGHEST, preferred_element_type=f32)
        own = tuple(mine[d] for d in dims)
        full[own] = done.astype(bf16)
        for phase in (2, 1, 0):
            d = dims[phase]
            lead = own[:phase]
            slab = full.at[own[: phase + 1]]
            if d == "y":
                copy = remote(slab, slab, mate)
                yield
                copy.wait_recv()
                continue
            up, down = up_of(mine[d]), down_of(mine[d])
            dev_up, dev_down = rings[d][1:]

            def half_of(r, half):
                size = 64 if phase == 2 else SIZES[dims[phase + 1]]
                return full.at[(*lead, r, pl.ds(half * (size // 2), size // 2))]

            gp = remote(slab, slab, dev_up)
            gm = remote(slab, slab, dev_down)
            yield
            gp.wait_recv()
            block = half_of(down, 0)
            fp = remote(block, block, dev_up)
            gm.wait_recv()
            block = half_of(up, 1)
            fm = remote(block, block, dev_down)
            yield
            fp.wait_recv()
            fm.wait_recv()

    pl.semaphore_wait(barrier, 5)

    flows, offset = [], 0
    for slot, (dims, wide) in enumerate((*CHUNKS, GRAM)):
        bufs = scratch[6 * slot : 6 * slot + 6]
        flows.append(flow(slot, dims, wide, offset, bufs, fulls[slot] if slot < n else None))
        offset += wide
    for slot in ORDER:
        next(flows[slot], None)
    for copy in sent:
        copy.wait_send()


def gathered_shape(dims, wide):
    return (*(SIZES[d] for d in dims), 64, wide)


def dp_part(turned, slopes, precond, squares):
    n = len(CHUNKS)
    bf = jnp.bfloat16
    vmem = pl.BlockSpec(memory_space=pltpu.VMEM)
    dma = pltpu.SemaphoreType.DMA
    scratch = []
    for dims, wide in (*CHUNKS, GRAM):
        scratch += chunk_scratch(dims, wide)
    shapes = [gathered_shape(dims, wide) for dims, wide in CHUNKS]
    *gathered, gram = pl.pallas_call(
        dp_kernel,
        out_shape=(*(pltpu.VMEM(shape, bf) for shape in shapes), pltpu.VMEM((64, 64), jnp.float32)),
        in_specs=[vmem] * 4,
        out_specs=(*(vmem for _ in shapes), vmem),
        scratch_shapes=[dma((n + 1, 26)), dma((n + 1, 26)), *scratch],
        compiler_params=pltpu.CompilerParams(
            collective_id=1, has_side_effects=True, vmem_limit_bytes=32 * 1024 * 1024
        ),
        name="dp_part",
    )(turned, slopes, precond, squares)
    return gathered, gram


def restore_kernel(owner_ref, *refs):
    n = len(CHUNKS)
    sources, gram_ref, dst_ref, gram_out, sem, gram_sem = refs[:n], *refs[n:]
    gram_copy = pltpu.make_async_copy(gram_ref, gram_out, gram_sem)
    gram_copy.start()

    def first(b, carry):
        o = owner_ref[b]
        at = {"z": o // 8, "x": (o // 2) % 4, "y": o % 2}
        offset = 0
        for c, (dims, wide) in enumerate(CHUNKS):
            src = sources[c].at[tuple(at[d] for d in dims)]
            pltpu.make_async_copy(src, dst_ref.at[b, :, pl.ds(offset, wide)], sem).start()
            offset += wide
        return carry

    lax.fori_loop(0, 32, first, 0, unroll=4)
    pltpu.make_async_copy(dst_ref, dst_ref, sem).wait()
    gram_copy.wait()


def restore(gathered, gram, owner):
    n = len(CHUNKS)
    width = sum(wide for _, wide in CHUNKS)
    hbm = pl.BlockSpec(memory_space=pl.ANY)
    return pl.pallas_call(
        restore_kernel,
        out_shape=(
            jax.ShapeDtypeStruct((32, 64, width), jnp.bfloat16),
            jax.ShapeDtypeStruct(gram.shape, gram.dtype),
        ),
        in_specs=[pl.BlockSpec(memory_space=pltpu.SMEM), *[pl.BlockSpec(memory_space=pltpu.VMEM)] * (n + 1)],
        out_specs=(hbm, hbm),
        scratch_shapes=[
            pltpu.SemaphoreType.DMA(()),
            pltpu.SemaphoreType.DMA(()),
        ],
        compiler_params=pltpu.CompilerParams(vmem_limit_bytes=16 * 1024 * 1024),
        name="restore",
    )(owner, *gathered, gram)


def body(inputs, cotangent, weights, preconds, order, owner):
    width = inputs.shape[2]
    turned, slopes, squares = relay(inputs, cotangent, weights, order[0], owner)
    gathered, gram = dp_part(turned, slopes, preconds[0, 0], squares)
    result, gram = restore(gathered, gram, owner)
    result = result.reshape(1, width, width)
    return (result, gram.reshape(1, 1, *gram.shape))


def solution(mesh):
    placed = (
        P(None, "dp", None),
        P(None, "dp", None),
        P("section", None, None),
        P("section", "dp", None, None),
        P("dp", None),
        P(),
    )
    return jax.shard_map(
        body,
        mesh=mesh,
        in_specs=placed,
        out_specs=(P("section", None, None), P("section", "dp", None, None)),
        check_vma=False,
    )
```

```python
import functools

import jax
import jax.numpy as jnp
from jax import lax
from jax.experimental import pallas as pl
from jax.experimental.pallas import tpu as pltpu
from jax.sharding import PartitionSpec as P

MESH = pl.DeviceIdType.MESH
coef = 0.7978845608028654
cubic = 0.044715


TILE = 512


def relay_kernel(
    order_ref,
    owner_ref,
    inputs_ref,
    cot_ref,
    weight_ref,
    turned_ref,
    dz,
    g_part,
    w,
    w_t,
    feed,
    held,
    slope,
    onward,
    grads,
    back,
    total,
    flipped,
    blocks_ref,
    w_sem,
    in_sem,
    f_send,
    f_recv,
    b_send,
    b_recv,
):
    s = lax.axis_index("section")
    n_micro, rows, width = held.shape
    n_tiles = width // TILE
    last = 3

    barrier = pltpu.get_barrier_semaphore()
    for dev in ((s + 1) % 4, (s + 3) % 4):
        pl.semaphore_signal(barrier, inc=1, device_id={"section": dev}, device_id_type=MESH)

    def find(p, carry):
        block = jnp.int32(0)
        for b in range(32):
            block = jnp.where(owner_ref[b] == p, jnp.int32(b), block)
        blocks_ref[p] = block
        return carry

    def tile(t):
        return slice(t * TILE, (t + 1) * TILE)

    def w_copy(t):
        return pltpu.make_async_copy(weight_ref.at[0, tile(t)], w.at[tile(t)], w_sem.at[t])

    feed_copy = pltpu.make_async_copy(inputs_ref, feed, in_sem)
    cot_copy = pltpu.make_async_copy(cot_ref, grads, in_sem)

    @pl.when(s == 0)
    def _():
        feed_copy.start()

    for t in range(n_tiles):
        w_copy(t).start()

    @pl.when(s == last)
    def _():
        cot_copy.start()

    g_part[...] = jnp.zeros(g_part.shape, g_part.dtype)
    lax.fori_loop(0, 32, find, 0)
    pl.semaphore_wait(barrier, 2)

    @pl.when(s == 0)
    def _():
        feed_copy.wait()

    @pl.when(s == last)
    def _():
        cot_copy.wait()

    def forward_copy(k, t):
        return pltpu.make_async_remote_copy(
            src_ref=onward.at[k, :, tile(t)],
            dst_ref=held.at[k, :, tile(t)],
            send_sem=f_send.at[k, t],
            recv_sem=f_recv.at[k, t],
            device_id={"section": (s + 1) % 4},
            device_id_type=MESH,
        )

    def backward_copy(k, t):
        return pltpu.make_async_remote_copy(
            src_ref=back.at[k, :, tile(t)],
            dst_ref=grads.at[k, :, tile(t)],
            send_sem=b_send.at[k, t],
            recv_sem=b_recv.at[k, t],
            device_id={"section": (s + 3) % 4},
            device_id_type=MESH,
        )

    def turn_weight():
        def strip(r, carry):
            at = pl.ds(pl.multiple_of(r * 256, 256), 256)
            for c in range(width // 256):
                cols = slice(c * 256, (c + 1) * 256)
                w_t[cols, at] = w[at, cols].T
            return carry

        lax.fori_loop(0, width // 256, strip, 0)

    def forward(k):
        @pl.when(s == 0)
        def _():
            held[k] = feed[order_ref[k]]

        for j in range(n_tiles):

            @pl.when(s > 0)
            def _():
                forward_copy(k, j).wait_recv()

            @pl.when((k == 0) & (s < 2))
            def _():
                w_copy(j).wait()

            for t in range(n_tiles):
                z = jnp.dot(held[k, :, tile(j)], w[tile(j), tile(t)], preferred_element_type=jnp.float32)
                if j > 0:
                    z = z + total[:, tile(t)]
                if j < n_tiles - 1:
                    total[:, tile(t)] = z
                    continue
                square = z * z
                tanh_part = jnp.tanh(coef * (z + cubic * square * z))
                half = 0.5 * (1.0 + tanh_part)
                before = held[k, :, tile(t)].astype(jnp.float32)
                onward[k, :, tile(t)] = (before + z * half).astype(jnp.bfloat16)

                @pl.when(s < last)
                def _():
                    forward_copy(k, t).start()

                slope[k, :, tile(t)] = half + 0.5 * z * (1.0 - tanh_part * tanh_part) * coef * (
                    1.0 + 3.0 * cubic * square
                )

    def backward(k):
        for j in range(n_tiles):

            @pl.when(s < last)
            def _():
                backward_copy(k, j).wait_recv()

            g = grads[k, :, tile(j)].astype(jnp.float32)
            piece = (g * slope[k, :, tile(j)]).astype(jnp.bfloat16)
            dz[k, :, tile(j)] = piece

            @pl.when(s > 0)
            def _():
                for t in range(n_tiles):
                    value = jnp.dot(
                        dz[k, :, tile(j)], w_t[tile(j), tile(t)], preferred_element_type=jnp.float32
                    )
                    if j > 0:
                        value = value + total[:, tile(t)]
                    if j < n_tiles - 1:
                        total[:, tile(t)] = value
                        continue
                    g = grads[k, :, tile(t)].astype(jnp.float32)
                    back[k, :, tile(t)] = (g + value).astype(jnp.bfloat16)
                    backward_copy(k, t).start()

    def turn(k):
        for part in range(8):
            block = held[k, :, part * 256 : (part + 1) * 256].T
            flipped[part * 4 : (part + 1) * 4] = block.reshape(4, 64, rows)

        lanes = pl.ds(pl.multiple_of(k * rows, rows), rows)

        def move(p, carry):
            turned_ref[p // 8, (p // 2) % 4, p % 2, :, lanes] = flipped[blocks_ref[p]]
            return carry

        lax.fori_loop(0, 32, move, 0)

    def squares():
        for z in range(4):
            for pair in range(2):
                left = turned_ref[z, pair * 2 : pair * 2 + 2].reshape(256, n_micro * rows)
                square = lax.dot_general(left, left, (((1,), (1,)), ((), ())), preferred_element_type=jnp.float32)
                for i in range(4):
                    lanes = slice(i * 64, (i + 1) * 64)
                    value = square[lanes, lanes].astype(jnp.bfloat16)
                    g_part[pair * 2 + i // 2, z // 2, z % 2, i % 2, :, 0:64] = value

    def step(k, carry):
        @pl.when(k < n_micro)
        def _():
            forward(k)

        @pl.when((k == n_micro - 1) & (s == 1))
        def _():
            turn_weight()

        b = k - jnp.where(s < 2, last, last - s)

        @pl.when((b >= 0) & (b < n_micro))
        def _():
            backward(b)

        @pl.when(k < n_micro)
        def _():
            turn(k)

        @pl.when(k == n_micro - 1)
        def _():
            squares()

        return carry

    @pl.when(s >= 2)
    def _():
        for t in range(n_tiles):
            w_copy(t).wait()
        turn_weight()

    lax.fori_loop(0, n_micro + last, step, 0)

    def drain(k, carry):
        @pl.when(s < last)
        def _():
            for t in range(n_tiles):
                forward_copy(k, t).wait_send()

        @pl.when(s > 0)
        def _():
            for t in range(n_tiles):
                backward_copy(k, t).wait_send()

        return carry

    lax.fori_loop(0, n_micro, drain, 0)


def relay(inputs, cotangent, weights, order, owner):
    n_micro, rows, width = inputs.shape
    n_tiles = width // TILE
    bf = jnp.bfloat16
    hbm, vmem = pl.BlockSpec(memory_space=pl.ANY), pl.BlockSpec(memory_space=pltpu.VMEM)
    smem = pl.BlockSpec(memory_space=pltpu.SMEM)
    block = pltpu.VMEM((n_micro, rows, width), bf)
    dma = pltpu.SemaphoreType.DMA
    return pl.pallas_call(
        relay_kernel,
        out_shape=(
            pltpu.VMEM((4, 4, 2, 64, n_micro * rows), bf),
            block,
            pltpu.VMEM(ring_shape(GRAM[0], GRAM[1]), bf),
        ),
        in_specs=[smem, smem, hbm, hbm, hbm],
        out_specs=(vmem, vmem, vmem),
        scratch_shapes=[
            pltpu.VMEM((width, width), bf),
            pltpu.VMEM((width, width), bf),
            block,
            block,
            pltpu.VMEM((n_micro, rows, width), jnp.float32),
            block,
            block,
            block,
            pltpu.VMEM((rows, width), jnp.float32),
            pltpu.VMEM((32, 64, rows), bf),
            pltpu.SMEM((32,), jnp.int32),
            dma((n_tiles,)),
            dma(()),
            dma((n_micro, n_tiles)),
            dma((n_micro, n_tiles)),
            dma((n_micro, n_tiles)),
            dma((n_micro, n_tiles)),
        ],
        compiler_params=pltpu.CompilerParams(
            collective_id=0, has_side_effects=True, vmem_limit_bytes=57 * 1024 * 1024
        ),
        name="relay",
    )(order, owner, inputs, cotangent, weights)


SIZES = {"x": 4, "z": 4, "y": 2}
CHUNKS = (("yxz", 256), ("yzx", 256), ("xzy", 256), ("zxy", 256), ("xzy", 256), ("zxy", 256), ("xzy", 256), ("zxy", 256))
GRAM = ("xzy", 128)
ORDER = (8, 7, 6, 0, 7, 6, 5, 2, 1, 5, 6, 2, 7, 0, 3, 2, 7, 6, 5, 0, 4, 3, 5, 7, 0, 1, 6, 7, 0, 4, 2, 8, 6, 1, 5, 0, 6, 7, 1, 0, 4, 3, 6, 7, 2, 1, 0, 5, 8, 3, 4, 7, 1, 8, 5, 4, 2, 3, 0, 1, 6, 2, 4, 7, 3, 8, 5, 1, 0, 4, 3, 8, 6, 2, 1, 3, 4, 2, 5, 4, 7, 3, 6, 1, 5, 2, 0, 4, 3, 2, 1, 5, 4, 3)


def ring_shape(dims, wide):
    if len(dims) == 1:
        return (4, 2, 32, wide)
    if dims[1] == "y":
        return (4, 2, *(SIZES[d] for d in dims[2:]), 64, wide)
    return (4, 2, 2, *(SIZES[d] for d in dims[2:]), 64, wide)


def phase_shapes(dims, wide):
    if dims[0] == "y":
        part = (2, *(SIZES[d] for d in dims[1:]), 64, wide)
        return part, part[1:]
    part = ring_shape(dims, wide)
    return part, (6, *part[2:])


def chunk_scratch(dims, wide):
    shapes = []
    for phase in range(3):
        shapes += phase_shapes(dims[phase:], wide)
    return [pltpu.VMEM(shape, jnp.bfloat16) for shape in shapes]


def dp_kernel(*refs):
    n = len(CHUNKS)
    h_p, dz_ref, pc_ref, squares_ref = refs[:4]
    fulls, gram_ref = refs[4 : 4 + n], refs[4 + n]
    send_sem, recv_sem = refs[5 + n : 7 + n]
    scratch = refs[7 + n :]
    scratch[6 * n][...] = squares_ref[...]

    me = lax.axis_index("dp")
    my_z, my_x, my_y = me // 8, (me // 2) % 4, me % 2

    def place(z, x, y):
        return z * 8 + x * 2 + y

    up_of, down_of, far_of = (lambda v: (v + 1) % 4), (lambda v: (v + 3) % 4), (lambda v: (v + 2) % 4)
    rings = {
        "x": (my_x, place(my_z, up_of(my_x), my_y), place(my_z, down_of(my_x), my_y)),
        "z": (my_z, place(up_of(my_z), my_x, my_y), place(down_of(my_z), my_x, my_y)),
    }
    mine = {"x": my_x, "z": my_z, "y": my_y}
    mate = place(my_z, my_x, 1 - my_y)

    barrier = pltpu.get_barrier_semaphore()
    for dev in (*rings["x"][1:], *rings["z"][1:], mate):
        pl.semaphore_signal(barrier, inc=1, device_id={"dp": dev}, device_id_type=MESH)

    rows = h_p.shape[-1]
    sent = []
    f32, bf16 = jnp.float32, jnp.bfloat16

    def left_rows(first, r, half_dim, half):
        if half_dim == "y":
            return (slice(None), r, half) if first == "x" else (r, slice(None), half)
        two = slice(2 * half, 2 * half + 2)
        return (two, r) if first == "x" else (r, two)

    def flow(slot, dims, wide, offset, bufs, full):
        cols = slice(offset, offset + wide)
        counter = [0]

        def remote(src, dst, dev):
            k = counter[0]
            counter[0] += 1
            copy = pltpu.make_async_remote_copy(
                src_ref=src,
                dst_ref=dst,
                send_sem=send_sem.at[slot, k],
                recv_sem=recv_sem.at[slot, k],
                device_id={"dp": dev},
                device_id_type=MESH,
            )
            copy.start()
            sent.append(copy)
            return copy

        def product(part, index, left):
            right = dz_ref[:, :, cols].reshape(rows, wide)
            value = jnp.dot(h_p[left].reshape(256, rows), right, preferred_element_type=f32)
            part[index] = value.astype(bf16).reshape(part.shape[len(index) :])

        def no_product(part, index, left):
            pass

        make = product if full is not None else no_product

        def store(part, ring_half, total):
            if ring_half is None:
                part[...] = total.astype(bf16).reshape(part.shape)
                return
            share = part.shape[0] // 2
            if share == 1:
                part[ring_half] = total.astype(bf16).reshape(part.shape[1:])
            else:
                where = slice(share * ring_half, share * ring_half + share)
                part[where] = total.astype(bf16).reshape(share, *part.shape[1:])

        total = None
        for phase in range(3):
            d = dims[phase]
            part, landed = bufs[2 * phase], bufs[2 * phase + 1]
            then = bufs[2 * phase + 2] if phase < 2 else None
            m = mine[d]
            if d == "y":
                other = 1 - my_y
                if phase == 0:
                    first = dims[1]
                    left = lambda r, y: (slice(None), r, y) if first == "x" else (r, slice(None), y)
                    copies = []
                    for r in range(4):
                        make(part, (other, r), left(r, other))
                        copies.append(remote(part.at[other, r], landed.at[r], mate))
                    for r in range(4):
                        make(part, (my_y, r), left(r, my_y))
                    yield
                    for r in range(4):
                        copies[r].wait_recv()
                        value = part[my_y, r].astype(f32) + landed[r].astype(f32)
                        then[r] = value.astype(bf16).reshape(then.shape[1:])
                else:
                    copy = remote(part.at[other], landed, mate)
                    yield
                    copy.wait_recv()
                    total = part[my_y].astype(f32) + landed[...].astype(f32)
                    if then is not None:
                        store(then, None, total)
                continue
            up, down, far = up_of(m), down_of(m), far_of(m)
            dev_up, dev_down = rings[d][1:]
            half_dim = dims[phase + 1] if phase < 2 else None
            fill = make if phase == 0 else no_product
            left = (lambda r, h: left_rows(d, r, half_dim, h)) if phase == 0 else (lambda r, h: None)
            fill(part, (far, 0), left(far, 0))
            mp = remote(part.at[far, 0], landed.at[0], dev_up)
            fill(part, (far, 1), left(far, 1))
            mm = remote(part.at[far, 1], landed.at[1], dev_down)
            fill(part, (up, 1), left(up, 1))
            dp = remote(part.at[up, 1], landed.at[2], dev_up)
            fill(part, (down, 0), left(down, 0))
            dm = remote(part.at[down, 0], landed.at[3], dev_down)
            fill(part, (up, 0), left(up, 0))
            fill(part, (down, 1), left(down, 1))
            yield
            mp.wait_recv()
            part[up, 0] = (part[up, 0].astype(f32) + landed[0].astype(f32)).astype(bf16)
            tp = remote(part.at[up, 0], landed.at[4], dev_up)
            mm.wait_recv()
            part[down, 1] = (part[down, 1].astype(f32) + landed[1].astype(f32)).astype(bf16)
            tm = remote(part.at[down, 1], landed.at[5], dev_down)
            fill(part, (m, 0), left(m, 0))
            fill(part, (m, 1), left(m, 1))
            yield
            halves = []
            for copy in (dp, dm, tp, tm):
                copy.wait_recv()
            for half, a, b in ((0, 3, 4), (1, 2, 5)):
                value = part[m, half].astype(f32) + landed[a].astype(f32) + landed[b].astype(f32)
                if then is not None:
                    store(then, half, value)
                halves.append(value)
            if then is None:
                total = jnp.concatenate(halves, axis=0)

        if full is None:
            gram_ref[...] = total[:, 0:64] * (1.0 / 16384.0)
            return
        done = jnp.dot(pc_ref[...], total, precision=lax.Precision.HIGHEST, preferred_element_type=f32)
        own = tuple(mine[d] for d in dims)
        full[own] = done.astype(bf16)
        for phase in (2, 1, 0):
            d = dims[phase]
            lead = own[:phase]
            slab = full.at[own[: phase + 1]]
            if d == "y":
                copy = remote(slab, slab, mate)
                yield
                copy.wait_recv()
                continue
            up, down = up_of(mine[d]), down_of(mine[d])
            dev_up, dev_down = rings[d][1:]

            def half_of(r, half):
                size = 64 if phase == 2 else SIZES[dims[phase + 1]]
                return full.at[(*lead, r, pl.ds(half * (size // 2), size // 2))]

            gp = remote(slab, slab, dev_up)
            gm = remote(slab, slab, dev_down)
            yield
            gp.wait_recv()
            block = half_of(down, 0)
            fp = remote(block, block, dev_up)
            gm.wait_recv()
            block = half_of(up, 1)
            fm = remote(block, block, dev_down)
            yield
            fp.wait_recv()
            fm.wait_recv()

    pl.semaphore_wait(barrier, 5)

    flows, offset = [], 0
    for slot, (dims, wide) in enumerate((*CHUNKS, GRAM)):
        bufs = scratch[6 * slot : 6 * slot + 6]
        flows.append(flow(slot, dims, wide, offset, bufs, fulls[slot] if slot < n else None))
        offset += wide
    for slot in ORDER:
        next(flows[slot], None)
    for copy in sent:
        copy.wait_send()


def gathered_shape(dims, wide):
    return (*(SIZES[d] for d in dims), 64, wide)


def dp_part(turned, slopes, precond, squares):
    n = len(CHUNKS)
    bf = jnp.bfloat16
    vmem = pl.BlockSpec(memory_space=pltpu.VMEM)
    dma = pltpu.SemaphoreType.DMA
    scratch = []
    for dims, wide in (*CHUNKS, GRAM):
        scratch += chunk_scratch(dims, wide)
    shapes = [gathered_shape(dims, wide) for dims, wide in CHUNKS]
    *gathered, gram = pl.pallas_call(
        dp_kernel,
        out_shape=(*(pltpu.VMEM(shape, bf) for shape in shapes), pltpu.VMEM((64, 64), jnp.float32)),
        in_specs=[vmem] * 4,
        out_specs=(*(vmem for _ in shapes), vmem),
        scratch_shapes=[dma((n + 1, 26)), dma((n + 1, 26)), *scratch],
        compiler_params=pltpu.CompilerParams(
            collective_id=1, has_side_effects=True, vmem_limit_bytes=32 * 1024 * 1024
        ),
        name="dp_part",
    )(turned, slopes, precond, squares)
    return gathered, gram


def restore_kernel(owner_ref, *refs):
    n = len(CHUNKS)
    sources, gram_ref, dst_ref, gram_out, sem, gram_sem = refs[:n], *refs[n:]
    gram_copy = pltpu.make_async_copy(gram_ref, gram_out, gram_sem)
    gram_copy.start()

    def first(b, carry):
        o = owner_ref[b]
        at = {"z": o // 8, "x": (o // 2) % 4, "y": o % 2}
        offset = 0
        for c, (dims, wide) in enumerate(CHUNKS):
            src = sources[c].at[tuple(at[d] for d in dims)]
            pltpu.make_async_copy(src, dst_ref.at[b, :, pl.ds(offset, wide)], sem).start()
            offset += wide
        return carry

    lax.fori_loop(0, 32, first, 0, unroll=4)
    pltpu.make_async_copy(dst_ref, dst_ref, sem).wait()
    gram_copy.wait()


def restore(gathered, gram, owner):
    n = len(CHUNKS)
    width = sum(wide for _, wide in CHUNKS)
    hbm = pl.BlockSpec(memory_space=pl.ANY)
    return pl.pallas_call(
        restore_kernel,
        out_shape=(
            jax.ShapeDtypeStruct((32, 64, width), jnp.bfloat16),
            jax.ShapeDtypeStruct(gram.shape, gram.dtype),
        ),
        in_specs=[pl.BlockSpec(memory_space=pltpu.SMEM), *[pl.BlockSpec(memory_space=pltpu.VMEM)] * (n + 1)],
        out_specs=(hbm, hbm),
        scratch_shapes=[
            pltpu.SemaphoreType.DMA(()),
            pltpu.SemaphoreType.DMA(()),
        ],
        compiler_params=pltpu.CompilerParams(vmem_limit_bytes=16 * 1024 * 1024),
        name="restore",
    )(owner, *gathered, gram)


def body(inputs, cotangent, weights, preconds, order, owner):
    width = inputs.shape[2]
    turned, slopes, squares = relay(inputs, cotangent, weights, order[0], owner)
    gathered, gram = dp_part(turned, slopes, preconds[0, 0], squares)
    result, gram = restore(gathered, gram, owner)
    result = result.reshape(1, width, width)
    return (result, gram.reshape(1, 1, *gram.shape))


def solution(mesh):
    placed = (
        P(None, "dp", None),
        P(None, "dp", None),
        P("section", None, None),
        P("section", "dp", None, None),
        P("dp", None),
        P(),
    )
    return jax.shard_map(
        body,
        mesh=mesh,
        in_specs=placed,
        out_specs=(P("section", None, None), P("section", "dp", None, None)),
        check_vma=False,
    )
```

```python
import functools

import jax
import jax.numpy as jnp
from jax import lax
from jax.experimental import pallas as pl
from jax.experimental.pallas import tpu as pltpu
from jax.sharding import PartitionSpec as P

MESH = pl.DeviceIdType.MESH
coef = 0.7978845608028654
cubic = 0.044715


TILE = 1024


def relay_kernel(
    order_ref,
    owner_ref,
    inputs_ref,
    cot_ref,
    weight_ref,
    turned_ref,
    dz,
    g_part,
    w,
    w_t,
    feed,
    held,
    slope,
    onward,
    grads,
    back,
    total,
    flipped,
    blocks_ref,
    w_sem,
    in_sem,
    f_send,
    f_recv,
    b_send,
    b_recv,
):
    s = lax.axis_index("section")
    n_micro, rows, width = held.shape
    n_tiles = width // TILE
    last = 3

    barrier = pltpu.get_barrier_semaphore()
    for dev in ((s + 1) % 4, (s + 3) % 4):
        pl.semaphore_signal(barrier, inc=1, device_id={"section": dev}, device_id_type=MESH)

    def find(p, carry):
        block = jnp.int32(0)
        for b in range(32):
            block = jnp.where(owner_ref[b] == p, jnp.int32(b), block)
        blocks_ref[p] = block
        return carry

    def tile(t):
        return slice(t * TILE, (t + 1) * TILE)

    def w_copy(t):
        return pltpu.make_async_copy(weight_ref.at[0, tile(t)], w.at[tile(t)], w_sem.at[t])

    feed_copy = pltpu.make_async_copy(inputs_ref, feed, in_sem)
    cot_copy = pltpu.make_async_copy(cot_ref, grads, in_sem)

    @pl.when(s == 0)
    def _():
        feed_copy.start()

    for t in range(n_tiles):
        w_copy(t).start()

    @pl.when(s == last)
    def _():
        cot_copy.start()

    g_part[...] = jnp.zeros(g_part.shape, g_part.dtype)
    lax.fori_loop(0, 32, find, 0)
    pl.semaphore_wait(barrier, 2)

    @pl.when(s == 0)
    def _():
        feed_copy.wait()

    @pl.when(s == last)
    def _():
        cot_copy.wait()

    def forward_copy(k, t):
        return pltpu.make_async_remote_copy(
            src_ref=onward.at[k, :, tile(t)],
            dst_ref=held.at[k, :, tile(t)],
            send_sem=f_send.at[k, t],
            recv_sem=f_recv.at[k, t],
            device_id={"section": (s + 1) % 4},
            device_id_type=MESH,
        )

    def backward_copy(k, t):
        return pltpu.make_async_remote_copy(
            src_ref=back.at[k, :, tile(t)],
            dst_ref=grads.at[k, :, tile(t)],
            send_sem=b_send.at[k, t],
            recv_sem=b_recv.at[k, t],
            device_id={"section": (s + 3) % 4},
            device_id_type=MESH,
        )

    def turn_weight():
        def strip(r, carry):
            at = pl.ds(pl.multiple_of(r * 256, 256), 256)
            for c in range(width // 256):
                cols = slice(c * 256, (c + 1) * 256)
                w_t[cols, at] = w[at, cols].T
            return carry

        lax.fori_loop(0, width // 256, strip, 0)

    def forward(k):
        @pl.when(s == 0)
        def _():
            held[k] = feed[order_ref[k]]

        for j in range(n_tiles):

            @pl.when(s > 0)
            def _():
                forward_copy(k, j).wait_recv()

            @pl.when((k == 0) & (s < 2))
            def _():
                w_copy(j).wait()

            for t in range(n_tiles):
                z = jnp.dot(held[k, :, tile(j)], w[tile(j), tile(t)], preferred_element_type=jnp.float32)
                if j > 0:
                    z = z + total[:, tile(t)]
                if j < n_tiles - 1:
                    total[:, tile(t)] = z
                    continue
                square = z * z
                tanh_part = jnp.tanh(coef * (z + cubic * square * z))
                half = 0.5 * (1.0 + tanh_part)
                before = held[k, :, tile(t)].astype(jnp.float32)
                onward[k, :, tile(t)] = (before + z * half).astype(jnp.bfloat16)

                @pl.when(s < last)
                def _():
                    forward_copy(k, t).start()

                slope[k, :, tile(t)] = half + 0.5 * z * (1.0 - tanh_part * tanh_part) * coef * (
                    1.0 + 3.0 * cubic * square
                )

    def backward(k):
        for j in range(n_tiles):

            @pl.when(s < last)
            def _():
                backward_copy(k, j).wait_recv()

            g = grads[k, :, tile(j)].astype(jnp.float32)
            piece = (g * slope[k, :, tile(j)]).astype(jnp.bfloat16)
            dz[k, :, tile(j)] = piece

            @pl.when(s > 0)
            def _():
                for t in range(n_tiles):
                    value = jnp.dot(
                        dz[k, :, tile(j)], w_t[tile(j), tile(t)], preferred_element_type=jnp.float32
                    )
                    if j > 0:
                        value = value + total[:, tile(t)]
                    if j < n_tiles - 1:
                        total[:, tile(t)] = value
                        continue
                    g = grads[k, :, tile(t)].astype(jnp.float32)
                    back[k, :, tile(t)] = (g + value).astype(jnp.bfloat16)
                    backward_copy(k, t).start()

    def turn(k):
        for part in range(8):
            block = held[k, :, part * 256 : (part + 1) * 256].T
            flipped[part * 4 : (part + 1) * 4] = block.reshape(4, 64, rows)

        lanes = pl.ds(pl.multiple_of(k * rows, rows), rows)

        def move(p, carry):
            turned_ref[p // 8, (p // 2) % 4, p % 2, :, lanes] = flipped[blocks_ref[p]]
            return carry

        lax.fori_loop(0, 32, move, 0)

    def squares():
        for z in range(4):
            for pair in range(2):
                left = turned_ref[z, pair * 2 : pair * 2 + 2].reshape(256, n_micro * rows)
                square = lax.dot_general(left, left, (((1,), (1,)), ((), ())), preferred_element_type=jnp.float32)
                for i in range(4):
                    lanes = slice(i * 64, (i + 1) * 64)
                    value = square[lanes, lanes].astype(jnp.bfloat16)
                    g_part[pair * 2 + i // 2, z // 2, z % 2, i % 2, :, 0:64] = value

    def step(k, carry):
        @pl.when(k < n_micro)
        def _():
            forward(k)

        @pl.when((k == n_micro - 1) & (s == 1))
        def _():
            turn_weight()

        b = k - jnp.where(s < 2, last, last - s)

        @pl.when((b >= 0) & (b < n_micro))
        def _():
            backward(b)

        @pl.when(k < n_micro)
        def _():
            turn(k)

        @pl.when(k == n_micro - 1)
        def _():
            squares()

        return carry

    @pl.when(s >= 2)
    def _():
        for t in range(n_tiles):
            w_copy(t).wait()
        turn_weight()

    lax.fori_loop(0, n_micro + last, step, 0)

    def drain(k, carry):
        @pl.when(s < last)
        def _():
            for t in range(n_tiles):
                forward_copy(k, t).wait_send()

        @pl.when(s > 0)
        def _():
            for t in range(n_tiles):
                backward_copy(k, t).wait_send()

        return carry

    lax.fori_loop(0, n_micro, drain, 0)


def relay(inputs, cotangent, weights, order, owner):
    n_micro, rows, width = inputs.shape
    n_tiles = width // TILE
    bf = jnp.bfloat16
    hbm, vmem = pl.BlockSpec(memory_space=pl.ANY), pl.BlockSpec(memory_space=pltpu.VMEM)
    smem = pl.BlockSpec(memory_space=pltpu.SMEM)
    block = pltpu.VMEM((n_micro, rows, width), bf)
    dma = pltpu.SemaphoreType.DMA
    return pl.pallas_call(
        relay_kernel,
        out_shape=(
            pltpu.VMEM((4, 4, 2, 64, n_micro * rows), bf),
            block,
            pltpu.VMEM(ring_shape(GRAM[0], GRAM[1]), bf),
        ),
        in_specs=[smem, smem, hbm, hbm, hbm],
        out_specs=(vmem, vmem, vmem),
        scratch_shapes=[
            pltpu.VMEM((width, width), bf),
            pltpu.VMEM((width, width), bf),
            block,
            block,
            pltpu.VMEM((n_micro, rows, width), jnp.float32),
            block,
            block,
            block,
            pltpu.VMEM((rows, width), jnp.float32),
            pltpu.VMEM((32, 64, rows), bf),
            pltpu.SMEM((32,), jnp.int32),
            dma((n_tiles,)),
            dma(()),
            dma((n_micro, n_tiles)),
            dma((n_micro, n_tiles)),
            dma((n_micro, n_tiles)),
            dma((n_micro, n_tiles)),
        ],
        compiler_params=pltpu.CompilerParams(
            collective_id=0, has_side_effects=True, vmem_limit_bytes=57 * 1024 * 1024
        ),
        name="relay",
    )(order, owner, inputs, cotangent, weights)


SIZES = {"x": 4, "z": 4, "y": 2}
CHUNKS = (("yxz", 256), ("yzx", 256), ("xzy", 256), ("zxy", 256), ("xzy", 256), ("zxy", 256), ("xzy", 256), ("zxy", 256))
GRAM = ("xzy", 128)
ORDER = (8, 7, 6, 0, 7, 6, 5, 2, 1, 5, 6, 2, 7, 0, 3, 2, 7, 6, 5, 0, 4, 3, 5, 7, 0, 1, 6, 7, 0, 4, 2, 8, 6, 1, 5, 0, 6, 7, 1, 0, 4, 3, 6, 7, 2, 1, 0, 5, 8, 3, 4, 7, 1, 8, 5, 4, 2, 3, 0, 1, 6, 2, 4, 7, 3, 8, 5, 1, 0, 4, 3, 8, 6, 2, 1, 3, 4, 2, 5, 4, 7, 3, 6, 1, 5, 2, 0, 4, 3, 2, 1, 5, 4, 3)


def ring_shape(dims, wide):
    if len(dims) == 1:
        return (4, 2, 32, wide)
    if dims[1] == "y":
        return (4, 2, *(SIZES[d] for d in dims[2:]), 64, wide)
    return (4, 2, 2, *(SIZES[d] for d in dims[2:]), 64, wide)


def phase_shapes(dims, wide):
    if dims[0] == "y":
        part = (2, *(SIZES[d] for d in dims[1:]), 64, wide)
        return part, part[1:]
    part = ring_shape(dims, wide)
    return part, (6, *part[2:])


def chunk_scratch(dims, wide):
    shapes = []
    for phase in range(3):
        shapes += phase_shapes(dims[phase:], wide)
    return [pltpu.VMEM(shape, jnp.bfloat16) for shape in shapes]


def dp_kernel(*refs):
    n = len(CHUNKS)
    h_p, dz_ref, pc_ref, squares_ref = refs[:4]
    fulls, gram_ref = refs[4 : 4 + n], refs[4 + n]
    send_sem, recv_sem = refs[5 + n : 7 + n]
    scratch = refs[7 + n :]
    scratch[6 * n][...] = squares_ref[...]

    me = lax.axis_index("dp")
    my_z, my_x, my_y = me // 8, (me // 2) % 4, me % 2

    def place(z, x, y):
        return z * 8 + x * 2 + y

    up_of, down_of, far_of = (lambda v: (v + 1) % 4), (lambda v: (v + 3) % 4), (lambda v: (v + 2) % 4)
    rings = {
        "x": (my_x, place(my_z, up_of(my_x), my_y), place(my_z, down_of(my_x), my_y)),
        "z": (my_z, place(up_of(my_z), my_x, my_y), place(down_of(my_z), my_x, my_y)),
    }
    mine = {"x": my_x, "z": my_z, "y": my_y}
    mate = place(my_z, my_x, 1 - my_y)

    barrier = pltpu.get_barrier_semaphore()
    for dev in (*rings["x"][1:], *rings["z"][1:], mate):
        pl.semaphore_signal(barrier, inc=1, device_id={"dp": dev}, device_id_type=MESH)

    rows = h_p.shape[-1]
    sent = []
    f32, bf16 = jnp.float32, jnp.bfloat16

    def left_rows(first, r, half_dim, half):
        if half_dim == "y":
            return (slice(None), r, half) if first == "x" else (r, slice(None), half)
        two = slice(2 * half, 2 * half + 2)
        return (two, r) if first == "x" else (r, two)

    def flow(slot, dims, wide, offset, bufs, full):
        cols = slice(offset, offset + wide)
        counter = [0]

        def remote(src, dst, dev):
            k = counter[0]
            counter[0] += 1
            copy = pltpu.make_async_remote_copy(
                src_ref=src,
                dst_ref=dst,
                send_sem=send_sem.at[slot, k],
                recv_sem=recv_sem.at[slot, k],
                device_id={"dp": dev},
                device_id_type=MESH,
            )
            copy.start()
            sent.append(copy)
            return copy

        def product(part, index, left):
            right = dz_ref[:, :, cols].reshape(rows, wide)
            value = jnp.dot(h_p[left].reshape(256, rows), right, preferred_element_type=f32)
            part[index] = value.astype(bf16).reshape(part.shape[len(index) :])

        def no_product(part, index, left):
            pass

        make = product if full is not None else no_product

        def store(part, ring_half, total):
            if ring_half is None:
                part[...] = total.astype(bf16).reshape(part.shape)
                return
            share = part.shape[0] // 2
            if share == 1:
                part[ring_half] = total.astype(bf16).reshape(part.shape[1:])
            else:
                where = slice(share * ring_half, share * ring_half + share)
                part[where] = total.astype(bf16).reshape(share, *part.shape[1:])

        total = None
        for phase in range(3):
            d = dims[phase]
            part, landed = bufs[2 * phase], bufs[2 * phase + 1]
            then = bufs[2 * phase + 2] if phase < 2 else None
            m = mine[d]
            if d == "y":
                other = 1 - my_y
                if phase == 0:
                    first = dims[1]
                    left = lambda r, y: (slice(None), r, y) if first == "x" else (r, slice(None), y)
                    copies = []
                    for r in range(4):
                        make(part, (other, r), left(r, other))
                        copies.append(remote(part.at[other, r], landed.at[r], mate))
                    for r in range(4):
                        make(part, (my_y, r), left(r, my_y))
                    yield
                    for r in range(4):
                        copies[r].wait_recv()
                        value = part[my_y, r].astype(f32) + landed[r].astype(f32)
                        then[r] = value.astype(bf16).reshape(then.shape[1:])
                else:
                    copy = remote(part.at[other], landed, mate)
                    yield
                    copy.wait_recv()
                    total = part[my_y].astype(f32) + landed[...].astype(f32)
                    if then is not None:
                        store(then, None, total)
                continue
            up, down, far = up_of(m), down_of(m), far_of(m)
            dev_up, dev_down = rings[d][1:]
            half_dim = dims[phase + 1] if phase < 2 else None
            fill = make if phase == 0 else no_product
            left = (lambda r, h: left_rows(d, r, half_dim, h)) if phase == 0 else (lambda r, h: None)
            fill(part, (far, 0), left(far, 0))
            mp = remote(part.at[far, 0], landed.at[0], dev_up)
            fill(part, (far, 1), left(far, 1))
            mm = remote(part.at[far, 1], landed.at[1], dev_down)
            fill(part, (up, 1), left(up, 1))
            dp = remote(part.at[up, 1], landed.at[2], dev_up)
            fill(part, (down, 0), left(down, 0))
            dm = remote(part.at[down, 0], landed.at[3], dev_down)
            fill(part, (up, 0), left(up, 0))
            fill(part, (down, 1), left(down, 1))
            yield
            mp.wait_recv()
            part[up, 0] = (part[up, 0].astype(f32) + landed[0].astype(f32)).astype(bf16)
            tp = remote(part.at[up, 0], landed.at[4], dev_up)
            mm.wait_recv()
            part[down, 1] = (part[down, 1].astype(f32) + landed[1].astype(f32)).astype(bf16)
            tm = remote(part.at[down, 1], landed.at[5], dev_down)
            fill(part, (m, 0), left(m, 0))
            fill(part, (m, 1), left(m, 1))
            yield
            halves = []
            for copy in (dp, dm, tp, tm):
                copy.wait_recv()
            for half, a, b in ((0, 3, 4), (1, 2, 5)):
                value = part[m, half].astype(f32) + landed[a].astype(f32) + landed[b].astype(f32)
                if then is not None:
                    store(then, half, value)
                halves.append(value)
            if then is None:
                total = jnp.concatenate(halves, axis=0)

        if full is None:
            gram_ref[...] = total[:, 0:64] * (1.0 / 16384.0)
            return
        done = jnp.dot(pc_ref[...], total, precision=lax.Precision.HIGHEST, preferred_element_type=f32)
        own = tuple(mine[d] for d in dims)
        full[own] = done.astype(bf16)
        for phase in (2, 1, 0):
            d = dims[phase]
            lead = own[:phase]
            slab = full.at[own[: phase + 1]]
            if d == "y":
                copy = remote(slab, slab, mate)
                yield
                copy.wait_recv()
                continue
            up, down = up_of(mine[d]), down_of(mine[d])
            dev_up, dev_down = rings[d][1:]

            def half_of(r, half):
                size = 64 if phase == 2 else SIZES[dims[phase + 1]]
                return full.at[(*lead, r, pl.ds(half * (size // 2), size // 2))]

            gp = remote(slab, slab, dev_up)
            gm = remote(slab, slab, dev_down)
            yield
            gp.wait_recv()
            block = half_of(down, 0)
            fp = remote(block, block, dev_up)
            gm.wait_recv()
            block = half_of(up, 1)
            fm = remote(block, block, dev_down)
            yield
            fp.wait_recv()
            fm.wait_recv()

    pl.semaphore_wait(barrier, 5)

    flows, offset = [], 0
    for slot, (dims, wide) in enumerate((*CHUNKS, GRAM)):
        bufs = scratch[6 * slot : 6 * slot + 6]
        flows.append(flow(slot, dims, wide, offset, bufs, fulls[slot] if slot < n else None))
        offset += wide
    for slot in ORDER:
        next(flows[slot], None)
    for copy in sent:
        copy.wait_send()


def gathered_shape(dims, wide):
    return (*(SIZES[d] for d in dims), 64, wide)


def dp_part(turned, slopes, precond, squares):
    n = len(CHUNKS)
    bf = jnp.bfloat16
    vmem = pl.BlockSpec(memory_space=pltpu.VMEM)
    dma = pltpu.SemaphoreType.DMA
    scratch = []
    for dims, wide in (*CHUNKS, GRAM):
        scratch += chunk_scratch(dims, wide)
    shapes = [gathered_shape(dims, wide) for dims, wide in CHUNKS]
    *gathered, gram = pl.pallas_call(
        dp_kernel,
        out_shape=(*(pltpu.VMEM(shape, bf) for shape in shapes), pltpu.VMEM((64, 64), jnp.float32)),
        in_specs=[vmem] * 4,
        out_specs=(*(vmem for _ in shapes), vmem),
        scratch_shapes=[dma((n + 1, 26)), dma((n + 1, 26)), *scratch],
        compiler_params=pltpu.CompilerParams(
            collective_id=1, has_side_effects=True, vmem_limit_bytes=32 * 1024 * 1024
        ),
        name="dp_part",
    )(turned, slopes, precond, squares)
    return gathered, gram


def restore_kernel(owner_ref, *refs):
    n = len(CHUNKS)
    sources, gram_ref, dst_ref, gram_out, sem, gram_sem = refs[:n], *refs[n:]
    gram_copy = pltpu.make_async_copy(gram_ref, gram_out, gram_sem)
    gram_copy.start()

    def first(b, carry):
        o = owner_ref[b]
        at = {"z": o // 8, "x": (o // 2) % 4, "y": o % 2}
        offset = 0
        for c, (dims, wide) in enumerate(CHUNKS):
            src = sources[c].at[tuple(at[d] for d in dims)]
            pltpu.make_async_copy(src, dst_ref.at[b, :, pl.ds(offset, wide)], sem).start()
            offset += wide
        return carry

    lax.fori_loop(0, 32, first, 0, unroll=4)
    pltpu.make_async_copy(dst_ref, dst_ref, sem).wait()
    gram_copy.wait()


def restore(gathered, gram, owner):
    n = len(CHUNKS)
    width = sum(wide for _, wide in CHUNKS)
    hbm = pl.BlockSpec(memory_space=pl.ANY)
    return pl.pallas_call(
        restore_kernel,
        out_shape=(
            jax.ShapeDtypeStruct((32, 64, width), jnp.bfloat16),
            jax.ShapeDtypeStruct(gram.shape, gram.dtype),
        ),
        in_specs=[pl.BlockSpec(memory_space=pltpu.SMEM), *[pl.BlockSpec(memory_space=pltpu.VMEM)] * (n + 1)],
        out_specs=(hbm, hbm),
        scratch_shapes=[
            pltpu.SemaphoreType.DMA(()),
            pltpu.SemaphoreType.DMA(()),
        ],
        compiler_params=pltpu.CompilerParams(vmem_limit_bytes=16 * 1024 * 1024),
        name="restore",
    )(owner, *gathered, gram)


def body(inputs, cotangent, weights, preconds, order, owner):
    width = inputs.shape[2]
    turned, slopes, squares = relay(inputs, cotangent, weights, order[0], owner)
    gathered, gram = dp_part(turned, slopes, preconds[0, 0], squares)
    result, gram = restore(gathered, gram, owner)
    result = result.reshape(1, width, width)
    return (result, gram.reshape(1, 1, *gram.shape))


def solution(mesh):
    placed = (
        P(None, "dp", None),
        P(None, "dp", None),
        P("section", None, None),
        P("section", "dp", None, None),
        P("dp", None),
        P(),
    )
    return jax.shard_map(
        body,
        mesh=mesh,
        in_specs=placed,
        out_specs=(P("section", None, None), P("section", "dp", None, None)),
        check_vma=False,
    )
```
